256 devices in a mesh: tm: 8 (over z_hi, core), space: 32 (over z_lo, x, y).
Axes of the slice: x: 4, y: 4, z: 8 (z_hi: 4, z_lo: 2; z = z_hi * 2 + z_lo), core: 2. Of those that a mesh axis runs over, the one named last changes fastest.
Arguments:
- nodes: float32 [8, 3, 256, 128, 128], P('tm', None, 'space'), may hold values from -1 to 1
- mobility: float32 [256, 128, 128], P('space'), may hold values from 0.03 to 0.15
- reaction: float32 [256, 128, 128], P('space'), may hold values from 0.2 to 1.5
Outputs:
- updated: float32 [8, 3, 256, 128, 128], P('tm', None, 'space')
The draws below stay inside these ranges and needn't reach their ends.
All inputs are finite; a program needn't handle non-finite values.
Results may differ from the reference program's by a relative error of at most 0.00002.
Values sent between devices are 32-bit elements; how exact they have to be, the bound alone decides.
No kernel may reach another device: no remote copies, remote signals or barrier semaphores. Data moves between devices by JAX's collectives and lax.ppermute only.
A program may use at most 64 MiB of HBM per device.

```python
import math
import jax
import jax.numpy as jnp
from jax import lax

NY = 128
NZ = 128
NX = 256
N_TM = 8


def levels(rng, dims, pieces, least, largest):
    def one(dim, blocks):
        steps = jax.random.uniform(jax.random.fold_in(jax.random.fold_in(rng, 6), dim), (blocks,), jnp.float32, least / len(pieces), largest / len(pieces))
        return jnp.repeat(jnp.exp(steps), dims[dim] // blocks).reshape((-1,) + (1,) * (len(dims) - dim - 1))

    loudness = one(*pieces[0])
    for cut in pieces[1:]:
        loudness = loudness * one(*cut)
    return loudness


def setup_inputs(seed: int = 0) -> dict:
    streams_of = jax.random.split(jax.random.key(seed), 4)
    nodes = jnp.clip(jax.random.uniform(streams_of[0], (N_TM, 3, NX, NY, NZ), jnp.float32, -1.0, 1.0) * levels(streams_of[0], (N_TM, 3, NX, NY, NZ), ((0, 8), (2, 32)), -0.4, 0.0), -1.0, 1.0)
    mobility = jnp.clip(jnp.exp(math.log(0.15) - 1.609438 * jax.random.uniform(streams_of[1], (NX, NY, NZ), jnp.float32) ** levels(streams_of[1], (NX, NY, NZ), ((0, 32),), -0.2, 0.2)), 0.03, 0.15)
    reaction = jnp.clip(jnp.exp(math.log(1.5) - 2.014903 * jax.random.uniform(streams_of[2], (NX, NY, NZ), jnp.float32) ** levels(streams_of[2], (NX, NY, NZ), ((0, 32),), -0.2, 0.2)), 0.2, 1.5)
    return dict(nodes=nodes, mobility=mobility, reaction=reaction)


substep = 0.5
edge_weight = 5.0 / 24.0
middle_weight = 1.0 / 3.0
far_weight = -1.0 / 24.0


def fine_force(field, mobility, reaction):
    neighbours = jnp.roll(field, -1, 1) + jnp.roll(field, 1, 1)
    neighbours = neighbours + jnp.roll(field, -1, 2) + jnp.roll(field, 1, 2)
    neighbours = neighbours + jnp.roll(field, -1, 3) + jnp.roll(field, 1, 3)
    return mobility * (neighbours - 6.0 * field) + reaction * (field - field * field * field)


def coarse_force(field, mob_coarse, rea_coarse):
    planar = jnp.roll(field, -1, 1) + jnp.roll(field, 1, 1) + jnp.roll(field, -1, 2) + jnp.roll(field, 1, 2)
    vertical = jnp.roll(field, -1, 3) + jnp.roll(field, 1, 3)
    diffusion = 0.25 * (planar - 4.0 * field) + (vertical - 2.0 * field)
    return mob_coarse * diffusion + rea_coarse * (field - field * field * field)


def integrals(first_force, second_force, third_force):
    leading = edge_weight * first_force + middle_weight * second_force + far_weight * third_force
    trailing = far_weight * first_force + middle_weight * second_force + edge_weight * third_force
    return leading, trailing


def restrict_axis(values, axis):
    evens = lax.slice_in_dim(values, 0, values.shape[axis], 2, axis)
    odds = lax.slice_in_dim(values, 1, values.shape[axis], 2, axis)
    return 0.5 * evens + 0.25 * (odds + jnp.roll(odds, 1, axis))


def prolong_axis(values, axis):
    upper = 0.5 * (values + jnp.roll(values, -1, axis))
    stacked = jnp.stack([values, upper], axis + 1)
    shape = list(values.shape)
    shape[axis] = shape[axis] * 2
    return stacked.reshape(shape)


def reference(nodes, mobility, reaction):
    mob_coarse = mobility[::2, ::2, :]
    rea_coarse = reaction[::2, ::2, :]
    swept_all = []
    coarse_all = []
    terms_all = []
    for slice_index in range(N_TM):
        states = nodes[slice_index]
        old = fine_force(states, mobility, reaction)
        first, second = integrals(old[0], old[1], old[2])
        start = states[0]
        node_one = start + first
        force_one = fine_force(node_one[None], mobility, reaction)[0]
        node_two = node_one + substep * (force_one - old[1]) + second
        force_two = fine_force(node_two[None], mobility, reaction)[0]
        new_first, new_second = integrals(old[0], force_one, force_two)
        stacked = jnp.stack([start, node_one, node_two, new_first, new_second])
        restricted = restrict_axis(restrict_axis(stacked, 2), 1)
        coarse = restricted[:3]
        coarse_old = coarse_force(coarse, mob_coarse, rea_coarse)
        terms = restricted[3:] - substep * coarse_old[:2]
        swept_all.append(jnp.stack([start, node_one, node_two]))
        coarse_all.append(coarse)
        terms_all.append(terms)
    initial = coarse_all[0][0]
    results = []
    previous_end = swept_all[0][0]
    for slice_index in range(N_TM):
        terms = terms_all[slice_index]
        level_one = initial + substep * coarse_force(initial[None], mob_coarse, rea_coarse)[0] + terms[0]
        level_two = level_one + substep * coarse_force(level_one[None], mob_coarse, rea_coarse)[0] + terms[1]
        difference = jnp.stack([level_one, level_two]) - coarse_all[slice_index][1:]
        correction = prolong_axis(prolong_axis(difference, 2), 1)
        corrected = swept_all[slice_index][1:] + correction
        if slice_index == 0:
            head = swept_all[0][0]
        else:
            head = previous_end
        results.append(jnp.stack([head, corrected[0], corrected[1]]))
        previous_end = corrected[1]
        initial = level_two
    return jnp.stack(results)
```

```python
import functools
import jax
import jax.numpy as jnp
from jax import lax
from jax.experimental import pallas as pl
from jax.experimental.pallas import tpu as pltpu
from jax.sharding import PartitionSpec as P

edge = 5.0 / 24.0
middle = 1.0 / 3.0
far = -1.0 / 24.0
substep = 0.5

VMEM = pltpu.CompilerParams(vmem_limit_bytes=40 * 1024 * 1024)


def roll(values, amount, axis):
    return pltpu.roll(values, amount % values.shape[axis], axis)


def around(values):
    return roll(values, 1, 0) + roll(values, -1, 0) + roll(values, 1, 1) + roll(values, -1, 1)


def cubic(values):
    return values - values * values * values


def cost(flops, moved):
    return pl.CostEstimate(flops=flops, bytes_accessed=moved, transcendentals=0)


def ring(values, axis, distance):
    count = lax.axis_size(axis)
    return lax.ppermute(values, axis, [(i, (i + distance) % count) for i in range(count)])


def swapped(values):
    count = lax.axis_size("tm")
    return lax.ppermute(values, "tm", [(i, i ^ 1) for i in range(count)])


def call(kernel, outs, scratch, *args, flops=10**6, scalars=0):
    moved = sum(a.size * 4 for a in args) + sum(4 * functools.reduce(lambda x, y: x * y, s) for s in outs)
    result = pl.pallas_call(
        kernel,
        out_shape=[jax.ShapeDtypeStruct(s, jnp.float32) for s in outs],
        in_specs=[pl.BlockSpec(memory_space=pltpu.SMEM)] * scalars
        + [pl.BlockSpec(memory_space=pltpu.VMEM)] * (len(args) - scalars),
        out_specs=[pl.BlockSpec(memory_space=pltpu.VMEM) for _ in outs],
        scratch_shapes=[pltpu.VMEM(s, jnp.float32) for s in scratch],
        compiler_params=VMEM,
        cost_estimate=cost(flops, moved),
    )(*args)
    return result


def coefficient_kernel(mob, rea, own, rightward, leftward):
    half = mob.shape[1] // 2
    for plane in range(4):
        m = 0.125 * mob[2 * plane, pl.ds(0, half, stride=2), :]
        r = 0.5 * rea[2 * plane, pl.ds(0, half, stride=2), :]
        own[0, plane] = m
        own[1, plane] = r
        leftward[0, plane] = m
        leftward[1, plane] = r
        if plane > 0:
            rightward[0, plane - 1] = m
            rightward[1, plane - 1] = r


def fine_kernel(
    nodes, mob, rea, left, right,
    v1_out, v2_out, coarse, terms, rightward, leftward,
    u, mw, rw, ca, cb, v1, v2, step, f1, jj, mix,
):
    half = mob.shape[1] // 2
    for m in range(3):
        for i in range(3):
            u[m, i] = left[3 * m + i]
            u[m, 11 + i] = right[3 * m + i]
    for i in range(2):
        mw[i] = left[9 + i]
        mw[10 + i] = right[9 + i]
        rw[i] = left[11 + i]
        rw[10 + i] = right[11 + i]

    @pl.loop(0, 8)
    def _(i):
        for m in range(3):
            u[m, i + 3] = nodes[m, i]
        mw[i + 2] = mob[i]
        rw[i + 2] = rea[i]

    @pl.loop(0, 14)
    def _(i):
        u0, u1, u2 = u[0, i], u[1, i], u[2, i]
        ca[i] = edge * u0 + middle * u1 + far * u2
        cb[i] = far * u0 + (middle - substep) * u1 + edge * u2

    @pl.loop(0, 12)
    def _(i):
        c0, c1, c2 = cubic(u[0, i + 1]), cubic(u[1, i + 1]), cubic(u[2, i + 1])
        a = ca[i + 1]
        b = cb[i + 1]
        lap_a = ca[i] + ca[i + 2] + around(a) - 6.0 * a
        lap_b = cb[i] + cb[i + 2] + around(b) - 6.0 * b
        v1[i] = u[0, i + 1] + mw[i] * lap_a + rw[i] * (edge * c0 + middle * c1 + far * c2)
        step[i] = mw[i] * lap_b + rw[i] * (far * c0 + (middle - substep) * c1 + edge * c2)

    @pl.loop(0, 10)
    def _(i):
        a = v1[i + 1]
        force = mw[i + 1] * (v1[i] + v1[i + 2] + around(a) - 6.0 * a) + rw[i + 1] * cubic(a)
        f1[i] = force
        v2[i] = a + (substep * force + step[i + 1])

    @pl.loop(0, 8)
    def _(i):
        a = v2[i + 1]
        b = u[0, i + 3]
        mm = mw[i + 2]
        rr = rw[i + 2]
        force = mm * (v2[i] + v2[i + 2] + around(a) - 6.0 * a) + rr * cubic(a)
        first = mm * (u[0, i + 2] + u[0, i + 4] + around(b) - 6.0 * b) + rr * cubic(b)
        second = middle * f1[i + 1]
        jj[0, i] = edge * first + second + far * force
        jj[1, i] = far * first + second + edge * force
        v1_out[i] = v1[i + 2]
        v2_out[i] = a

    def reduced(slot):
        even = mix[slot, pl.ds(0, half, stride=2), :]
        odd = mix[slot, pl.ds(1, half, stride=2), :]
        return 0.5 * even + 0.25 * (odd + roll(odd, 1, 0))

    @pl.loop(0, 4)
    def _(j):
        mix[0] = 0.5 * u[0, 2 * j + 3] + 0.25 * (u[0, 2 * j + 4] + u[0, 2 * j + 2])
        mix[1] = 0.5 * v1[2 * j + 2] + 0.25 * (v1[2 * j + 3] + v1[2 * j + 1])
        mix[2] = 0.5 * v2[2 * j + 1] + 0.25 * (v2[2 * j + 2] + v2[2 * j])
        before = jnp.maximum(2 * j - 1, 0)
        weight = jnp.where(j == 0, 0.0, 0.25)
        for m in range(2):
            mix[3 + m] = 0.5 * jj[m, 2 * j] + 0.25 * jj[m, 2 * j + 1] + weight * jj[m, before]
        for m in range(3):
            coarse[m, j] = reduced(m)
        for m in range(2):
            terms[m, j] = reduced(3 + m)

    for m in range(2):
        rightward[m] = coarse[m, 3]
        mix[m] = jj[m, 7]
        rightward[2 + m] = 0.25 * reduced(m)
    for m in range(3):
        leftward[m] = coarse[m, 0]


def half_force(mid, low, high, mob, rea):
    planar = low + high + roll(mid, 1, 0) + roll(mid, -1, 0)
    vertical = roll(mid, 1, 1) + roll(mid, -1, 1)
    return mob * (planar + 4.0 * vertical - 12.0 * mid) + rea * cubic(mid)


def term_kernel(coarse, terms, from_left, from_right, own, q, rightward, leftward, window):
    for m in range(2):
        window[m, 0] = from_left[m]
        window[m, 5] = from_right[m]
        for j in range(4):
            window[m, j + 1] = coarse[m, j]
    for m in range(2):
        for j in range(4):
            values = terms[m, j] - half_force(window[m, j + 1], window[m, j], window[m, j + 2], own[0, j], own[1, j])
            if j == 0:
                values = values + from_left[2 + m]
            q[4 * m + j] = values
            if m == 0:
                leftward[j] = values
                if j > 0:
                    rightward[j - 1] = values
            else:
                if j < 3:
                    leftward[4 + j] = values
                if j > 1:
                    rightward[1 + j] = values
    for j in range(4):
        rightward[5 + j] = coarse[0, j]
        leftward[7 + j] = window[0, j + 2]


def base_kernel(v1, v2, coarse, from_right, b1, b2, wide):
    half = coarse.shape[2]
    for m, v, b in ((1, v1, b1), (2, v2, b2)):
        widen(lambda j, m=m: coarse[m, j] if j < 4 else from_right[m], wide, half)
        for j in range(4):
            low = wide[j]
            b[2 * j] = v[2 * j] - low
            b[2 * j + 1] = v[2 * j + 1] - 0.5 * (low + wide[j + 1])


def widen(values, wide, half):
    for j in range(5):
        d = values(j)
        wide[j, pl.ds(0, half, stride=2), :] = d
        wide[j, pl.ds(1, half, stride=2), :] = 0.5 * (d + roll(d, -1, 0))


def pack_kernel(q, coarse, from_left, from_right, c_right, own, c_l, c_r, window, mw, rw):
    for i in range(3):
        window[i] = from_left[i]
        mw[i] = c_l[0, i]
        rw[i] = c_l[1, i]
    for i in range(4):
        window[3 + i] = q[i]
        window[7 + i] = from_right[i]
        mw[3 + i] = own[0, i]
        rw[3 + i] = own[1, i]
        mw[7 + i] = c_r[0, i]
        rw[7 + i] = c_r[1, i]
    for i in range(2):
        window[11 + i] = from_left[3 + i]
    for i in range(4):
        window[13 + i] = q[4 + i]
    for i in range(3):
        window[17 + i] = from_right[4 + i]
    for i in range(4):
        window[20 + i] = from_left[5 + i]
        window[24 + i] = coarse[0, i]
        window[29 + i] = from_right[7 + i]
    window[28] = c_right[0]


def sweep_kernel(first_turn, *refs):
    if first_turn:
        flags, mine, other, mw, rw, levels, last, x0, x1, x2, x3 = refs
    else:
        flags, mine, other, mw, rw, mid, low, high, levels, last, x0, x1, x2, x3 = refs

    def run(a, b):
        def own_start():
            @pl.loop(0, 13)
            def _(i):
                x0[i] = a[20 + i]

        if first_turn:
            own_start()
        else:
            pl.when(flags[1] == 0)(own_start)

            @pl.when(flags[1] != 0)
            def _():
                for i in range(4):
                    x0[i] = low[i]
                    x0[9 + i] = high[1 + i]
                for i in range(5):
                    x0[4 + i] = mid[i]

        @pl.loop(0, 11)
        def _(i):
            x1[i] = x0[i + 1] + half_force(x0[i + 1], x0[i], x0[i + 2], mw[i], rw[i]) + a[i]

        @pl.loop(0, 9)
        def _(i):
            x2[i] = x1[i + 1] + half_force(x1[i + 1], x1[i], x1[i + 2], mw[i + 1], rw[i + 1]) + a[11 + i]

        @pl.loop(0, 7)
        def _(i):
            x3[i] = x2[i + 1] + half_force(x2[i + 1], x2[i], x2[i + 2], mw[i + 2], rw[i + 2]) + b[2 + i]

        @pl.loop(0, 5)
        def _(i):
            end = x3[i + 1] + half_force(x3[i + 1], x3[i], x3[i + 2], mw[i + 3], rw[i + 3]) + b[13 + i]
            last[i] = end
            levels[0, i] = x0[i + 4]
            levels[1, i] = x1[i + 3]
            levels[2, i] = x2[i + 2]
            levels[3, i] = x3[i + 1]
            levels[4, i] = end

    pl.when(flags[0] == 0)(lambda: run(mine, other))
    pl.when(flags[0] != 0)(lambda: run(other, mine))


def final_kernel(flags, start, b1, b2, b_before, levels, out, wide):
    half = levels.shape[2]
    core = flags[0]
    for m, b in ((0, b_before), (1, b1), (2, b2)):

        def corrected(m=m, b=b):
            widen(lambda j: levels[2 * core + m, j], wide, half)
            for j in range(4):
                low = wide[j]
                out[0, m, 2 * j] = b[2 * j] + low
                out[0, m, 2 * j + 1] = b[2 * j + 1] + 0.5 * (low + wide[j + 1])

        if m == 0:
            pl.when(flags[2] != 0)(corrected)

            @pl.when(flags[2] == 0)
            def _():
                for i in range(8):
                    out[0, 0, i] = start[i]

        else:
            corrected()


def body(nodes, mobility, reaction):
    states = nodes[0]
    _, blocks, ny, nz = states.shape
    hy = ny // 2
    slice_index = lax.axis_index("tm")
    flags = jnp.stack([slice_index % 2, slice_index // 2, slice_index]).astype(jnp.int32)

    to_right = jnp.concatenate([states[:, 5:].reshape(9, ny, nz), mobility[6:], reaction[6:]])
    to_left = jnp.concatenate([states[:, :3].reshape(9, ny, nz), mobility[:2], reaction[:2]])
    left = ring(to_right, "space", 1)
    right = ring(to_left, "space", -1)

    own, c_to_right, c_to_left = call(
        coefficient_kernel, [(2, 4, hy, nz), (2, 3, hy, nz), (2, 4, hy, nz)], [], mobility, reaction
    )
    c_l = ring(c_to_right, "space", 1)
    c_r = ring(c_to_left, "space", -1)

    plane = (ny, nz)
    small = (hy, nz)
    v1, v2, coarse, terms, to_right, to_left = call(
        fine_kernel,
        [(8,) + plane, (8,) + plane, (3, 4) + small, (2, 4) + small, (4,) + small, (3,) + small],
        [(3, 14) + plane, (12,) + plane, (12,) + plane, (14,) + plane, (14,) + plane, (12,) + plane, (10,) + plane,
         (12,) + plane, (10,) + plane, (2, 8) + plane, (5,) + plane],
        states, mobility, reaction, left, right, flops=2 * 10**7,
    )
    from_left = ring(to_right, "space", 1)
    from_right = ring(to_left, "space", -1)
    q, to_right, to_left = call(
        term_kernel,
        [(8,) + small, (9,) + small, (11,) + small],
        [(2, 6) + small],
        coarse, terms, from_left, from_right, own,
    )
    q_left = ring(to_right, "space", 1)
    q_right = ring(to_left, "space", -1)
    b1, b2 = call(base_kernel, [(8,) + plane, (8,) + plane], [(5,) + plane], v1, v2, coarse, from_right)
    b_before = ring(b2, "tm", 1)
    mine, mw, rw = call(
        pack_kernel, [(33,) + small, (11,) + small, (11,) + small], [],
        q, coarse, q_left, q_right, from_right, own, c_l, c_r,
    )
    other = swapped(mine)
    sweep_outs = [(5, 5) + small, (5,) + small]
    sweep_scratch = [(13,) + small, (11,) + small, (9,) + small, (7,) + small]
    levels, last = call(
        functools.partial(sweep_kernel, True), sweep_outs, sweep_scratch, flags, mine, other, mw, rw, scalars=1
    )
    turns = lax.axis_size("tm") // 2
    for _ in range(turns - 1):
        mid = ring(last, "tm", 2)
        low = ring(mid, "space", 1)
        high = ring(mid, "space", -1)
        levels, last = call(
            functools.partial(sweep_kernel, False), sweep_outs, sweep_scratch,
            flags, mine, other, mw, rw, mid, low, high, scalars=1,
        )
    (out,) = call(
        final_kernel, [(1, 3, 8) + plane], [(5,) + plane], flags, states[0], b1, b2, b_before, levels, scalars=1
    )
    return out


def solution(mesh):
    return jax.shard_map(
        body,
        mesh=mesh,
        in_specs=(
            P("tm", None, "space", None, None),
            P("space", None, None),
            P("space", None, None),
        ),
        out_specs=P("tm", None, "space", None, None),
        check_vma=False,
    )
```

```python
import functools
import jax
import jax.numpy as jnp
from jax import lax
from jax.experimental import pallas as pl
from jax.experimental.pallas import tpu as pltpu
from jax.sharding import PartitionSpec as P

edge = 5.0 / 24.0
middle = 1.0 / 3.0
far = -1.0 / 24.0
substep = 0.5


def roll(values, amount, axis):
    return pltpu.roll(values, amount % values.shape[axis], axis)


def around(values):
    return roll(values, 1, 0) + roll(values, -1, 0) + roll(values, 1, 1) + roll(values, -1, 1)


def cubic(values):
    return values - values * values * values


def cost(flops, moved):
    return pl.CostEstimate(flops=flops, bytes_accessed=moved, transcendentals=0)


def ring(values, axis, distance):
    count = lax.axis_size(axis)
    return lax.ppermute(values, axis, [(i, (i + distance) % count) for i in range(count)])


def together(*values):
    return lax.optimization_barrier(values)


def swapped(values):
    count = lax.axis_size("tm")
    return lax.ppermute(values, "tm", [(i, i ^ 1) for i in range(count)])


def call(kernel, outs, scratch, *args, flops=10**6, scalars=0, limit=8):
    moved = sum(a.size * 4 for a in args) + sum(4 * functools.reduce(lambda x, y: x * y, s) for s in outs)
    result = pl.pallas_call(
        kernel,
        out_shape=[jax.ShapeDtypeStruct(s, jnp.float32) for s in outs],
        in_specs=[pl.BlockSpec(memory_space=pltpu.SMEM)] * scalars
        + [pl.BlockSpec(memory_space=pltpu.VMEM)] * (len(args) - scalars),
        out_specs=[pl.BlockSpec(memory_space=pltpu.VMEM) for _ in outs],
        scratch_shapes=[pltpu.VMEM(s, jnp.float32) for s in scratch],
        compiler_params=pltpu.CompilerParams(vmem_limit_bytes=limit * 1024 * 1024),
        cost_estimate=cost(flops, moved),
    )(*args)
    return result


def coefficient_kernel(mob, rea, own, rightward, leftward):
    half = mob.shape[1] // 2
    for k, (source, scale) in enumerate(((mob, 0.125), (rea, 0.5))):
        for j in range(4):
            own[k, j] = scale * source[2 * j, pl.ds(0, half, stride=2), :]
        for j in range(2):
            rightward[k, pl.ds(j * half, half), :] = own[k, j + 1]
        for j in range(3):
            place = 3 * k + j
            leftward[place // 2, pl.ds(place % 2 * half, half), :] = own[k, j + 1]


def window_kernel(own, left, right, mw, rw):
    half = own.shape[2]
    for k, (out, scale) in enumerate(((mw, 0.125), (rw, 0.5))):
        for j in range(2):
            out[j] = left[13 + k, pl.ds(j * half, half), :]
        out[2] = scale * left[9 + 2 * k, pl.ds(0, half, stride=2), :]
        for j in range(4):
            out[3 + j] = own[k, j]
        out[7] = scale * right[9 + 2 * k, pl.ds(0, half, stride=2), :]
        for j in range(3):
            place = 3 * k + j
            out[8 + j] = right[13 + place // 2, pl.ds(place % 2 * half, half), :]


def widen(d, wide, j):
    half = d.shape[0]
    wide[j, pl.ds(0, half, stride=2), :] = d
    wide[j, pl.ds(1, half, stride=2), :] = 0.5 * (d + roll(d, -1, 0))


def half_force(mid, low, high, mob, rea):
    planar = low + high + roll(mid, 1, 0) + roll(mid, -1, 0)
    vertical = roll(mid, 1, 1) + roll(mid, -1, 1)
    return mob * (planar + 4.0 * vertical - 12.0 * mid) + rea * cubic(mid)


def fine_kernel(
    nodes, mob, rea, left, right, own,
    b1, b2, q, start, coarse, share, rightward, leftward,
    u, mw, rw, ca, cb, v1, v2, step, f1, jj, mix,
):
    half = mob.shape[1] // 2
    for m in range(3):
        for i in range(3):
            u[m, i] = left[3 * m + i]
            u[m, 11 + i] = right[3 * m + i]
    for i in range(2):
        mw[i] = left[9 + i]
        mw[10 + i] = right[9 + i]
        rw[i] = left[11 + i]
        rw[10 + i] = right[11 + i]

    @pl.loop(0, 8)
    def _(i):
        for m in range(3):
            u[m, i + 3] = nodes[m, i]
        mw[i + 2] = mob[i]
        rw[i + 2] = rea[i]

    @pl.loop(0, 14)
    def _(i):
        u0, u1, u2 = u[0, i], u[1, i], u[2, i]
        ca[i] = edge * u0 + middle * u1 + far * u2
        cb[i] = far * u0 + (middle - substep) * u1 + edge * u2

    @pl.loop(0, 12)
    def _(i):
        c0, c1, c2 = cubic(u[0, i + 1]), cubic(u[1, i + 1]), cubic(u[2, i + 1])
        a = ca[i + 1]
        b = cb[i + 1]
        lap_a = ca[i] + ca[i + 2] + around(a) - 6.0 * a
        lap_b = cb[i] + cb[i + 2] + around(b) - 6.0 * b
        v1[i] = u[0, i + 1] + mw[i] * lap_a + rw[i] * (edge * c0 + middle * c1 + far * c2)
        step[i] = mw[i] * lap_b + rw[i] * (far * c0 + (middle - substep) * c1 + edge * c2)

    @pl.loop(0, 10)
    def _(i):
        a = v1[i + 1]
        force = mw[i + 1] * (v1[i] + v1[i + 2] + around(a) - 6.0 * a) + rw[i + 1] * cubic(a)
        f1[i] = force
        v2[i] = a + (substep * force + step[i + 1])

    @pl.loop(0, 8)
    def _(i):
        a = v2[i + 1]
        b = u[0, i + 3]
        mm = mw[i + 2]
        rr = rw[i + 2]
        force = mm * (v2[i] + v2[i + 2] + around(a) - 6.0 * a) + rr * cubic(a)
        first = mm * (u[0, i + 2] + u[0, i + 4] + around(b) - 6.0 * b) + rr * cubic(b)
        second = middle * f1[i + 1]
        jj[0, i] = edge * first + second + far * force
        jj[1, i] = far * first + second + edge * force

    def reduced(slot):
        even = mix[slot, pl.ds(0, half, stride=2), :]
        odd = mix[slot, pl.ds(1, half, stride=2), :]
        return 0.5 * even + 0.25 * (odd + roll(odd, 1, 0))

    @pl.loop(0, 6)
    def _(j):
        mix[0] = 0.5 * u[0, 2 * j + 1] + 0.25 * (u[0, 2 * j + 2] + u[0, 2 * j])
        start[j] = reduced(0)

    @pl.loop(0, 4)
    def _(j):
        mix[1] = 0.5 * v1[2 * j + 2] + 0.25 * (v1[2 * j + 3] + v1[2 * j + 1])
        mix[2] = 0.5 * v2[2 * j + 1] + 0.25 * (v2[2 * j + 2] + v2[2 * j])
        before = jnp.maximum(2 * j - 1, 0)
        weight = jnp.where(j == 0, 0.0, 0.25)
        for m in range(2):
            mix[3 + m] = 0.5 * jj[m, 2 * j] + 0.25 * jj[m, 2 * j + 1] + weight * jj[m, before]
        for m in range(2):
            coarse[m, j] = reduced(1 + m)
        for m in range(2):
            q[4 * m + j] = reduced(3 + m)

    for m in range(2):
        mix[m] = jj[m, 7]
        share[m] = 0.25 * reduced(m)

    empty = jnp.zeros_like(share[0])
    for j in range(4):
        q[j] = q[j] - half_force(start[j + 1], start[j], start[j + 2], own[0, j], own[1, j])
        low = coarse[0, j - 1] if j > 0 else empty
        high = coarse[0, j + 1] if j < 3 else empty
        q[4 + j] = q[4 + j] - half_force(coarse[0, j], low, high, own[0, j], own[1, j])

    for i in range(3):
        rightward[i] = q[1 + i]
        rightward[5 + i] = start[1 + i]
        leftward[4 + i] = q[4 + i]
    for i in range(2):
        rightward[3 + i] = q[6 + i]
        rightward[9 + i] = share[i]
        leftward[11 + i] = coarse[i, 0]
    rightward[8] = coarse[0, 3]
    for i in range(4):
        leftward[i] = q[i]
        leftward[7 + i] = start[2 + i]

    for m, v, first, b in ((0, v1, 2, b1), (1, v2, 1, b2)):
        for j in range(4):
            widen(coarse[m, j], mix, j)
        mix[4] = jnp.zeros_like(mix[4])
        for j in range(4):
            low = mix[j]
            b[2 * j] = v[2 * j + first] - low
            b[2 * j + 1] = v[2 * j + 1 + first] - 0.5 * (low + mix[j + 1])


def pack_kernel(q, start, c1, share, from_left, from_right, mw, window):
    window[0] = from_left[0]
    window[1] = from_left[1]
    window[2] = from_left[2]
    window[3] = q[0] + from_left[9]
    for i in range(1, 4):
        window[3 + i] = q[i]
        window[7 + i] = from_right[i]
    window[7] = from_right[0] + share[0]
    window[11] = from_left[3]
    window[12] = from_left[4] - mw[2] * c1[0]
    window[13] = q[4] + from_left[10] - mw[3] * from_left[8]
    window[14] = q[5]
    window[15] = q[6]
    window[16] = q[7] - mw[6] * from_right[11]
    window[17] = from_right[4] + share[1] - mw[7] * c1[3]
    window[18] = from_right[5]
    window[19] = from_right[6]
    for i in range(3):
        window[20 + i] = from_left[5 + i]
    for i in range(6):
        window[23 + i] = start[i]
    for i in range(4):
        window[29 + i] = from_right[7 + i]
    for i in range(2):
        window[33 + i] = from_right[11 + i]


def order(first, second, out):
    for i in range(20):
        out[i] = first[i]
    for i in range(7):
        out[20 + i] = second[2 + i]
    for i in range(5):
        out[27 + i] = second[13 + i]
    for i in range(2):
        out[32 + i] = first[33 + i]
        out[34 + i] = second[33 + i]
    for i in range(13):
        out[36 + i] = first[20 + i]


def sweep(x0, q, mw, rw, last, levels, x1, x2, x3):
    def level(source, target, count, terms, shift):
        for i in range(count):
            mid = source[i + 1]
            force = half_force(mid, source[i], source[i + 2], mw[i + shift], rw[i + shift])
            target[i] = mid + force + q[terms + i]

    level(x0, x1, 11, 0, 0)
    level(x1, x2, 9, 11, 1)
    level(x2, x3, 7, 20, 2)
    level(x3, last, 5, 27, 3)
    last[5] = q[35]
    if levels is not None:
        for i in range(4):
            levels[0, i] = x0[i + 4]
            levels[1, i] = x1[i + 3]
            levels[2, i] = x2[i + 2]
            levels[3, i] = x3[i + 1]
            levels[4, i] = last[i]
        levels[1, 4] = x1[7] - q[32]
        levels[2, 4] = x2[6] - q[33]
        levels[3, 4] = x3[5] - q[34]
        levels[4, 4] = last[4] - q[35]


def first_kernel(flags, mine, other, mw, rw, last, ordered, x1, x2, x3):
    pl.when(flags[0] == 0)(lambda: order(mine, other, ordered))
    pl.when(flags[0] != 0)(lambda: order(other, mine, ordered))
    sweep(ordered.at[pl.ds(36, 13)], ordered, mw, rw, last, None, x1, x2, x3)


def turn_kernel(final, flags, ordered, mw, rw, mid, low, high, last, *refs):
    levels = refs[0] if final else None
    x0, x1, x2, x3 = refs[-4:]

    @pl.when(flags[1] == 0)
    def _():
        for i in range(13):
            x0[i] = ordered[36 + i]

    @pl.when(flags[1] != 0)
    def _():
        for i in range(4):
            x0[i] = low[i]
            x0[9 + i] = high[i]
        for i in range(5):
            x0[4 + i] = mid[i]

    sweep(x0, ordered, mw, rw, last, levels, x1, x2, x3)
    if final:
        levels[0, 4] = mid[4] - mid[5]


def final_kernel(flags, start, b1, b2, b_before, levels, out, wide):
    core = flags[0]
    for m, b in ((0, b_before), (1, b1), (2, b2)):

        def corrected(m=m, b=b):
            for j in range(5):
                widen(levels[2 * core + m, j], wide, j)
            for j in range(4):
                low = wide[j]
                out[0, m, 2 * j] = b[2 * j] + low
                out[0, m, 2 * j + 1] = b[2 * j + 1] + 0.5 * (low + wide[j + 1])

        if m == 0:
            pl.when(flags[2] != 0)(corrected)

            @pl.when(flags[2] == 0)
            def _():
                for i in range(8):
                    out[0, 0, i] = start[i]

        else:
            corrected()


def body(nodes, mobility, reaction):
    states = nodes[0]
    _, blocks, ny, nz = states.shape
    hy = ny // 2
    plane = (ny, nz)
    small = (hy, nz)
    slice_index = lax.axis_index("tm")
    flags = jnp.stack([slice_index % 2, slice_index // 2, slice_index]).astype(jnp.int32)

    own, c_to_right, c_to_left = call(
        coefficient_kernel, [(2, 4) + small, (2,) + plane, (3,) + plane], [], mobility, reaction
    )
    to_right = jnp.concatenate([states[:, 5:].reshape((9,) + plane), mobility[6:], reaction[6:], c_to_right])
    to_left = jnp.concatenate([states[:, :3].reshape((9,) + plane), mobility[:2], reaction[:2], c_to_left])
    left = ring(to_right, "space", 1)
    right = ring(to_left, "space", -1)
    b1, b2, q, start, coarse, share, to_right, to_left = call(
        fine_kernel,
        [(8,) + plane, (8,) + plane, (8,) + small, (6,) + small, (2, 4) + small, (2,) + small, (11,) + small, (13,) + small],
        [(3, 14) + plane, (12,) + plane, (12,) + plane, (14,) + plane, (14,) + plane, (12,) + plane, (10,) + plane,
         (12,) + plane, (10,) + plane, (2, 8) + plane, (5,) + plane],
        states, mobility, reaction, left, right, own, flops=2 * 10**7, limit=16,
    )
    q_left = ring(to_right, "space", 1)
    q_right = ring(to_left, "space", -1)
    b_before = ring(b2, "tm", 1)
    mw, rw = call(window_kernel, [(11,) + small, (11,) + small], [], own, left, right)
    (mine,) = call(pack_kernel, [(35,) + small], [], q, start, coarse[0], share, q_left, q_right, mw)
    other = swapped(mine)
    levels_shape = [(11,) + small, (9,) + small, (7,) + small]
    last, ordered = call(
        first_kernel, [(6,) + small, (49,) + small], levels_shape, flags, mine, other, mw, rw, scalars=1
    )
    turns = lax.axis_size("tm") // 2
    for turn in range(1, turns):
        final = turn == turns - 1
        mid = ring(last, "tm", 2)
        if turn == 1:
            mid, b_before = together(mid, b_before)
        low = ring(mid[0:4], "space", 1)
        high = ring(mid[1:5], "space", -1)
        last, *levels = call(
            functools.partial(turn_kernel, final), [(6,) + small] + [(5, 5) + small] * final, [(13,) + small] + levels_shape,
            flags, ordered, mw, rw, mid, low, high, scalars=1,
        )
    (out,) = call(
        final_kernel, [(1, 3, 8) + plane], [(5,) + plane], flags, states[0], b1, b2, b_before, levels[0], scalars=1,
    )
    return out


def solution(mesh):
    return jax.shard_map(
        body,
        mesh=mesh,
        in_specs=(
            P("tm", None, "space", None, None),
            P("space", None, None),
            P("space", None, None),
        ),
        out_specs=P("tm", None, "space", None, None),
        check_vma=False,
    )
```

```python
import functools
import jax
import jax.numpy as jnp
from jax import lax
from jax.experimental import pallas as pl
from jax.experimental.pallas import tpu as pltpu
from jax.sharding import PartitionSpec as P

edge = 5.0 / 24.0
middle = 1.0 / 3.0
far = -1.0 / 24.0
substep = 0.5


def roll(values, amount, axis):
    return pltpu.roll(values, amount % values.shape[axis], axis)


def around(values):
    return roll(values, 1, 0) + roll(values, -1, 0) + roll(values, 1, 1) + roll(values, -1, 1)


def cubic(values):
    return values - values * values * values


def cost(flops, moved):
    return pl.CostEstimate(flops=flops, bytes_accessed=moved, transcendentals=0)


def ring(values, axis, distance):
    count = lax.axis_size(axis)
    return lax.ppermute(values, axis, [(i, (i + distance) % count) for i in range(count)])


def together(*values):
    return lax.optimization_barrier(values)


def swapped(values):
    count = lax.axis_size("tm")
    return lax.ppermute(values, "tm", [(i, i ^ 1) for i in range(count)])


def call(kernel, outs, scratch, *args, flops=10**6, scalars=0, limit=8):
    moved = sum(a.size * 4 for a in args) + sum(4 * functools.reduce(lambda x, y: x * y, s) for s in outs)
    result = pl.pallas_call(
        kernel,
        out_shape=[jax.ShapeDtypeStruct(s, jnp.float32) for s in outs],
        in_specs=[pl.BlockSpec(memory_space=pltpu.SMEM)] * scalars
        + [pl.BlockSpec(memory_space=pltpu.VMEM)] * (len(args) - scalars),
        out_specs=[pl.BlockSpec(memory_space=pltpu.VMEM) for _ in outs],
        scratch_shapes=[pltpu.VMEM(s, jnp.float32) for s in scratch],
        compiler_params=pltpu.CompilerParams(vmem_limit_bytes=limit * 1024 * 1024),
        cost_estimate=cost(flops, moved),
    )(*args)
    return result


def laplace(mid, *beside):
    total = around(mid) - 6.0 * mid
    for values in beside:
        total = total + values
    return total


def leading(x0, x1, x2):
    return edge * x0 + middle * x1 + far * x2


def trailing(x0, x1, x2):
    return far * x0 + (middle - substep) * x1 + edge * x2


def cubics(nodes, plane):
    return [cubic(nodes[m, plane]) for m in range(3)]


def edge_kernel(flags, nodes, mob, rea, own, rightward, leftward, mix):
    half = mob.shape[1] // 2
    for k, (source, scale) in enumerate(((mob, 0.125), (rea, 0.5))):
        for j in range(4):
            own[k, j] = scale * source[2 * j, pl.ds(0, half, stride=2), :]

    for core in range(2):

        @pl.when(flags[0] == core)
        def _():
            for j in range(3):
                for out in (rightward, leftward):
                    out[8 + j // 2, pl.ds(j % 2 * half, half), :] = own[core, j + 1]

    for out, outer, inner, third in ((rightward, 7, 6, 5), (leftward, 0, 1, 2)):
        lead = [leading(nodes[0, p], nodes[1, p], nodes[2, p]) for p in (outer, inner, third)]
        cubes = cubics(nodes, inner)
        out[0] = nodes[0, inner] + mob[inner] * laplace(lead[1], lead[0], lead[2]) + rea[inner] * leading(*cubes)
        cubes = cubics(nodes, outer)
        out[1] = nodes[0, outer] + mob[outer] * laplace(lead[0], lead[1]) + rea[outer] * leading(*cubes)
        out[4] = lead[0]
        trail = [trailing(nodes[0, p], nodes[1, p], nodes[2, p]) for p in (outer, inner)]
        out[2] = mob[outer] * laplace(trail[0], trail[1]) + rea[outer] * trailing(*cubes)
        out[5] = trail[0]
        out[3] = nodes[0, outer]
        out[6] = mob[outer]
        out[7] = rea[outer]
    mix[...] = 0.5 * nodes[0, 0] + 0.25 * nodes[0, 1]
    leftward[9, pl.ds(half, half), :] = reduced(mix)
    rightward[9, pl.ds(half, half), :] = jnp.zeros_like(own[0, 0])


def local_kernel(nodes, mob, rea, v1, step, first, lead, trail, start):
    for array in (lead, trail, start):
        for i in (0, 9):
            array[i] = jnp.zeros_like(array[i])

    @pl.loop(0, 8)
    def _(i):
        states = nodes[0, i], nodes[1, i], nodes[2, i]
        lead[i + 1] = leading(*states)
        trail[i + 1] = trailing(*states)
        start[i + 1] = states[0]

    @pl.loop(0, 8)
    def _(i):
        cubes = cubics(nodes, i)
        m = mob[i]
        r = rea[i]
        v1[i] = nodes[0, i] + m * laplace(lead[i + 1], lead[i], lead[i + 2]) + r * leading(*cubes)
        step[i] = m * laplace(trail[i + 1], trail[i], trail[i + 2]) + r * trailing(*cubes)
        first[i] = m * laplace(start[i + 1], start[i], start[i + 2]) + r * cubes[0]


def reduced(mix):
    half = mix.shape[0] // 2
    even = mix[pl.ds(0, half, stride=2), :]
    odd = mix[pl.ds(1, half, stride=2), :]
    return 0.5 * even + 0.25 * (odd + roll(odd, 1, 0))


def widen(d, wide, j):
    half = d.shape[0]
    wide[j, pl.ds(0, half, stride=2), :] = d
    wide[j, pl.ds(1, half, stride=2), :] = 0.5 * (d + roll(d, -1, 0))


def half_force(mid, low, high, mob, rea):
    planar = low + high + roll(mid, 1, 0) + roll(mid, -1, 0)
    vertical = roll(mid, 1, 1) + roll(mid, -1, 1)
    return mob * (planar + 4.0 * vertical - 12.0 * mid) + rea * cubic(mid)


def fine_kernel(
    nodes, mob, rea, left, right, to_right, to_left, own, v1_own, step_own, first_own,
    b1, b2, q, start, coarse, share, outer, rightward, leftward,
    mw, rw, v1, v2, step, first, f1, jj, mix,
):
    half = mob.shape[1] // 2

    @pl.loop(0, 8)
    def _(i):
        mw[i + 1] = mob[i]
        rw[i + 1] = rea[i]
        v1[i + 2] = v1_own[i]
        step[i + 1] = step_own[i]
        first[i] = first_own[i]

    for got, sent, place, far_place, beyond, plane in ((left, to_left, 1, 0, 0, 0), (right, to_right, 10, 11, 9, 7)):
        mw[beyond] = got[6]
        rw[beyond] = got[7]
        v1[far_place] = got[0]
        v1[place] = got[1] + got[6] * sent[4]
        step[beyond] = got[2] + got[6] * sent[5]
        v1[plane + 2] = v1_own[plane] + mob[plane] * got[4]
        step[plane + 1] = step_own[plane] + mob[plane] * got[5]
        first[plane] = first_own[plane] + mob[plane] * got[3]

    @pl.loop(0, 10, unroll=2)
    def _(i):
        a = v1[i + 1]
        force = mw[i] * laplace(a, v1[i], v1[i + 2]) + rw[i] * cubic(a)
        f1[i] = force
        v2[i] = a + (substep * force + step[i])

    @pl.loop(0, 8, unroll=2)
    def _(i):
        a = v2[i + 1]
        force = mob[i] * laplace(a, v2[i], v2[i + 2]) + rea[i] * cubic(a)
        second = middle * f1[i + 1]
        jj[0, i] = edge * first[i] + second + far * force
        jj[1, i] = far * first[i] + second + edge * force

    for j in range(4):
        before = nodes[0, 2 * j - 1] if j > 0 else left[3]
        mix[0] = 0.5 * nodes[0, 2 * j] + 0.25 * (nodes[0, 2 * j + 1] + before)
        mix[1] = 0.5 * v1[2 * j + 2] + 0.25 * (v1[2 * j + 3] + v1[2 * j + 1])
        mix[2] = 0.5 * v2[2 * j + 1] + 0.25 * (v2[2 * j + 2] + v2[2 * j])
        for m in range(2):
            mix[3 + m] = 0.5 * jj[m, 2 * j] + 0.25 * jj[m, 2 * j + 1]
            if j > 0:
                mix[3 + m] = mix[3 + m] + 0.25 * jj[m, 2 * j - 1]
        start[j] = reduced(mix.at[0])
        for m in range(2):
            coarse[m, j] = reduced(mix.at[1 + m])
            q[4 * m + j] = reduced(mix.at[3 + m])
    mix[0] = nodes[0, 7]
    start[4] = right[9, pl.ds(half, half), :] + 0.25 * reduced(mix.at[0])
    for m in range(2):
        mix[1 + m] = jj[m, 7]
        share[m] = 0.25 * reduced(mix.at[1 + m])

    outer[0] = 0.125 * right[6, pl.ds(0, half, stride=2), :]
    outer[1] = 0.5 * right[7, pl.ds(0, half, stride=2), :]
    for j in range(3):
        for side, got in enumerate((left, right)):
            outer[2 + 3 * side + j] = got[8 + j // 2, pl.ds(j % 2 * half, half), :]

    empty = jnp.zeros_like(share[0])
    for j in range(4):
        low = start[j - 1] if j > 0 else empty
        q[j] = q[j] - half_force(start[j], low, start[j + 1], own[0, j], own[1, j])
        low = coarse[0, j - 1] if j > 0 else empty
        high = coarse[0, j + 1] if j < 3 else empty
        q[4 + j] = q[4 + j] - half_force(coarse[0, j], low, high, own[0, j], own[1, j])

    for i in range(3):
        rightward[i] = q[1 + i]
        leftward[4 + i] = q[4 + i]
    for i in range(2):
        rightward[3 + i] = q[6 + i]
        rightward[10 + i] = share[i]
        leftward[11 + i] = coarse[i, 0]
    rightward[9] = coarse[0, 3]
    for i in range(4):
        rightward[5 + i] = start[i]
        leftward[i] = q[i]
        leftward[7 + i] = start[1 + i]

    for m, v, shift, b in ((0, v1, 2, b1), (1, v2, 1, b2)):
        for j in range(4):
            widen(coarse[m, j], mix, j)
        mix[4] = jnp.zeros_like(mix[4])
        for j in range(4):
            low = mix[j]
            b[2 * j] = v[2 * j + shift] - low
            b[2 * j + 1] = v[2 * j + 1 + shift] - 0.5 * (low + mix[j + 1])


def pack_kernel(q, start, c1, share, own, outer, from_left, from_right, window):
    window[0] = from_left[0]
    window[1] = from_left[1]
    window[2] = from_left[2]
    window[3] = q[0] + from_left[10] - own[0, 0] * from_left[8]
    for i in range(1, 4):
        window[3 + i] = q[i]
        window[7 + i] = from_right[i]
    window[7] = from_right[0] + share[0] - outer[0] * start[3]
    window[11] = from_left[3]
    window[12] = from_left[4]
    window[13] = q[4] + from_left[11] - own[0, 0] * from_left[9]
    window[14] = q[5]
    window[15] = q[6]
    window[16] = q[7] - own[0, 3] * from_right[11]
    window[17] = from_right[4] + share[1] - outer[0] * c1[3]
    window[18] = from_right[5]
    window[19] = from_right[6]
    for i in range(4):
        window[20 + i] = from_left[5 + i]
        window[29 + i] = from_right[7 + i]
    for i in range(5):
        window[24 + i] = start[i]
    for i in range(2):
        window[33 + i] = from_right[11 + i]
    for i in range(6):
        window[35 + i] = outer[2 + i]
    window[41] = c1[0]


def order(first, second, own, outer, out, mw, rw):
    for k, (source, coefficient) in enumerate(((first, mw), (second, rw))):
        for i in range(3):
            coefficient[i] = source[35 + i]
            coefficient[8 + i] = source[38 + i]
        for i in range(4):
            coefficient[3 + i] = own[k, i]
        coefficient[7] = outer[k]
    for i in range(20):
        out[i] = first[i]
    out[12] = first[12] - mw[2] * first[41]
    for i in range(7):
        out[20 + i] = second[2 + i]
    for i in range(5):
        out[27 + i] = second[13 + i]
    for i in range(2):
        out[32 + i] = first[33 + i]
        out[34 + i] = second[33 + i]
    for i in range(13):
        out[36 + i] = first[20 + i]


def sweep(x0, q, mw, rw, last, levels, x1, x2, x3):
    def level(source, target, count, terms, shift):
        for i in range(count):
            mid = source[i + 1]
            force = half_force(mid, source[i], source[i + 2], mw[i + shift], rw[i + shift])
            target[i] = mid + force + q[terms + i]

    level(x0, x1, 11, 0, 0)
    level(x1, x2, 9, 11, 1)
    level(x2, x3, 7, 20, 2)
    level(x3, last, 5, 27, 3)
    last[5] = q[35]
    if levels is not None:
        for i in range(4):
            levels[0, i] = x0[i + 4]
            levels[1, i] = x1[i + 3]
            levels[2, i] = x2[i + 2]
            levels[3, i] = x3[i + 1]
            levels[4, i] = last[i]
        levels[1, 4] = x1[7] - q[32]
        levels[2, 4] = x2[6] - q[33]
        levels[3, 4] = x3[5] - q[34]
        levels[4, 4] = last[4] - q[35]


def first_kernel(flags, mine, other, own, outer, last, ordered, mw, rw, x1, x2, x3):
    pl.when(flags[0] == 0)(lambda: order(mine, other, own, outer, ordered, mw, rw))
    pl.when(flags[0] != 0)(lambda: order(other, mine, own, outer, ordered, mw, rw))
    sweep(ordered.at[pl.ds(36, 13)], ordered, mw, rw, last, None, x1, x2, x3)


def turn_kernel(final, flags, ordered, mw, rw, mid, low, high, last, *refs):
    levels = refs[0] if final else None
    x0, x1, x2, x3 = refs[-4:]

    @pl.when(flags[1] == 0)
    def _():
        for i in range(13):
            x0[i] = ordered[36 + i]

    @pl.when(flags[1] != 0)
    def _():
        for i in range(4):
            x0[i] = low[i]
            x0[9 + i] = high[i]
        for i in range(5):
            x0[4 + i] = mid[i]

    sweep(x0, ordered, mw, rw, last, levels, x1, x2, x3)
    if final:
        levels[0, 4] = mid[4] - mid[5]


def final_kernel(flags, start, b1, b2, b_before, levels, out, wide):
    core = flags[0]
    for m, b in ((0, b_before), (1, b1), (2, b2)):

        def corrected(m=m, b=b):
            for j in range(5):
                widen(levels[2 * core + m, j], wide, j)
            for j in range(4):
                low = wide[j]
                out[0, m, 2 * j] = b[2 * j] + low
                out[0, m, 2 * j + 1] = b[2 * j + 1] + 0.5 * (low + wide[j + 1])

        if m == 0:
            pl.when(flags[2] != 0)(corrected)

            @pl.when(flags[2] == 0)
            def _():
                for i in range(8):
                    out[0, 0, i] = start[i]

        else:
            corrected()


def body(nodes, mobility, reaction):
    states = nodes[0]
    _, blocks, ny, nz = states.shape
    hy = ny // 2
    plane = (ny, nz)
    small = (hy, nz)
    slice_index = lax.axis_index("tm")
    flags = jnp.stack([slice_index % 2, slice_index // 2, slice_index]).astype(jnp.int32)

    own, to_right, to_left = call(
        edge_kernel, [(2, 4) + small, (10,) + plane, (10,) + plane], [plane], flags, states, mobility, reaction, scalars=1
    )
    left = ring(to_right, "space", 1)
    right = ring(to_left, "space", -1)
    v1, step, first = call(
        local_kernel, [(8,) + plane] * 3, [(10,) + plane] * 3, states, mobility, reaction, flops=10**7
    )
    b1, b2, q, start, coarse, share, outer, to_right, to_left = call(
        fine_kernel,
        [(8,) + plane, (8,) + plane, (8,) + small, (5,) + small, (2, 4) + small, (2,) + small, (8,) + small, (12,) + small,
         (13,) + small],
        [(10,) + plane, (10,) + plane, (12,) + plane, (10,) + plane, (10,) + plane, (8,) + plane, (10,) + plane,
         (2, 8) + plane, (5,) + plane],
        states, mobility, reaction, left, right, to_right, to_left, own, v1, step, first, flops=2 * 10**7, limit=16,
    )
    q_left = ring(to_right, "space", 1)
    q_right = ring(to_left, "space", -1)
    b_before = ring(b2, "tm", 1)
    (mine,) = call(pack_kernel, [(42,) + small], [], q, start, coarse[0], share, own, outer, q_left, q_right)
    other = swapped(mine)
    levels_shape = [(11,) + small, (9,) + small, (7,) + small]
    last, ordered, mw, rw = call(
        first_kernel, [(6,) + small, (49,) + small, (11,) + small, (11,) + small], levels_shape,
        flags, mine, other, own, outer, scalars=1,
    )
    turns = lax.axis_size("tm") // 2
    for turn in range(1, turns):
        final = turn == turns - 1
        mid = ring(last, "tm", 2)
        if turn == 1:
            mid, b_before = together(mid, b_before)
        low = ring(mid[0:4], "space", 1)
        high = ring(mid[1:5], "space", -1)
        last, *levels = call(
            functools.partial(turn_kernel, final), [(6,) + small] + [(5, 5) + small] * final, [(13,) + small] + levels_shape,
            flags, ordered, mw, rw, mid, low, high, scalars=1,
        )
    (out,) = call(
        final_kernel, [(1, 3, 8) + plane], [(5,) + plane], flags, states[0], b1, b2, b_before, levels[0], scalars=1,
    )
    return out


def solution(mesh):
    return jax.shard_map(
        body,
        mesh=mesh,
        in_specs=(
            P("tm", None, "space", None, None),
            P("space", None, None),
            P("space", None, None),
        ),
        out_specs=P("tm", None, "space", None, None),
        check_vma=False,
    )
```

```python
import functools
import jax
import jax.numpy as jnp
from jax import lax
from jax.experimental import pallas as pl
from jax.experimental.pallas import tpu as pltpu
from jax.sharding import PartitionSpec as P

edge = 5.0 / 24.0
middle = 1.0 / 3.0
far = -1.0 / 24.0
substep = 0.5


def roll(values, amount, axis):
    return pltpu.roll(values, amount % values.shape[axis], axis)


def around(values):
    return roll(values, 1, 0) + roll(values, -1, 0) + roll(values, 1, 1) + roll(values, -1, 1)


def cubic(values):
    return values - values * values * values


def cost(flops, moved):
    return pl.CostEstimate(flops=flops, bytes_accessed=moved, transcendentals=0)


def ring(values, axis, distance):
    count = lax.axis_size(axis)
    return lax.ppermute(values, axis, [(i, (i + distance) % count) for i in range(count)])


def together(*values):
    return lax.optimization_barrier(values)


def swapped(values):
    count = lax.axis_size("tm")
    return lax.ppermute(values, "tm", [(i, i ^ 1) for i in range(count)])


def call(kernel, outs, scratch, *args, flops=10**6, scalars=0, limit=8):
    moved = sum(a.size * 4 for a in args) + sum(4 * functools.reduce(lambda x, y: x * y, s) for s in outs)
    result = pl.pallas_call(
        kernel,
        out_shape=[jax.ShapeDtypeStruct(s, jnp.float32) for s in outs],
        in_specs=[pl.BlockSpec(memory_space=pltpu.SMEM)] * scalars
        + [pl.BlockSpec(memory_space=pltpu.VMEM)] * (len(args) - scalars),
        out_specs=[pl.BlockSpec(memory_space=pltpu.VMEM) for _ in outs],
        scratch_shapes=[pltpu.VMEM(s, jnp.float32) for s in scratch],
        compiler_params=pltpu.CompilerParams(vmem_limit_bytes=limit * 1024 * 1024),
        cost_estimate=cost(flops, moved),
    )(*args)
    return result


def laplace(mid, *beside):
    total = around(mid) - 6.0 * mid
    for values in beside:
        total = total + values
    return total


def leading(x0, x1, x2):
    return edge * x0 + middle * x1 + far * x2


def trailing(x0, x1, x2):
    return far * x0 + (middle - substep) * x1 + edge * x2


def cubics(nodes, plane):
    return [cubic(nodes[m, plane]) for m in range(3)]


def edge_kernel(flags, nodes_hbm, mob_hbm, rea_hbm, own, rightward, leftward, mix, nodes, mob, rea, sems):
    half = mob.shape[1] // 2
    copies = [pltpu.make_async_copy(mob_hbm, mob, sems.at[0]), pltpu.make_async_copy(rea_hbm, rea, sems.at[1])]
    for m in range(3):
        for k, first in enumerate((5, 0)):
            part = pl.ds(first, 3)
            copies.append(pltpu.make_async_copy(nodes_hbm.at[m, part], nodes.at[m, part], sems.at[2 + 2 * m + k]))
    for copy in copies:
        copy.start()
    for copy in copies[:2]:
        copy.wait()
    for k, (source, scale) in enumerate(((mob, 0.125), (rea, 0.5))):
        for j in range(4):
            own[k, j] = scale * source[2 * j, pl.ds(0, half, stride=2), :]

    for core in range(2):

        @pl.when(flags[0] == core)
        def _():
            for j in range(3):
                for out in (rightward, leftward):
                    out[8 + j // 2, pl.ds(j % 2 * half, half), :] = own[core, j + 1]

    for copy in copies[2:]:
        copy.wait()

    for out, outer, inner, third in ((rightward, 7, 6, 5), (leftward, 0, 1, 2)):
        lead = [leading(nodes[0, p], nodes[1, p], nodes[2, p]) for p in (outer, inner, third)]
        cubes = cubics(nodes, inner)
        out[0] = nodes[0, inner] + mob[inner] * laplace(lead[1], lead[0], lead[2]) + rea[inner] * leading(*cubes)
        cubes = cubics(nodes, outer)
        out[1] = nodes[0, outer] + mob[outer] * laplace(lead[0], lead[1]) + rea[outer] * leading(*cubes)
        out[4] = lead[0]
        trail = [trailing(nodes[0, p], nodes[1, p], nodes[2, p]) for p in (outer, inner)]
        out[2] = mob[outer] * laplace(trail[0], trail[1]) + rea[outer] * trailing(*cubes)
        out[5] = trail[0]
        out[3] = nodes[0, outer]
        out[6] = mob[outer]
        out[7] = rea[outer]
    mix[...] = 0.5 * nodes[0, 0] + 0.25 * nodes[0, 1]
    leftward[9, pl.ds(half, half), :] = reduced(mix)
    rightward[9, pl.ds(half, half), :] = jnp.zeros_like(own[0, 0])


def local_kernel(nodes, mob, rea, v1, step, first, lead, trail, start):
    for array in (lead, trail, start):
        for i in (0, 9):
            array[i] = jnp.zeros_like(array[i])

    @pl.loop(0, 8)
    def _(i):
        states = nodes[0, i], nodes[1, i], nodes[2, i]
        lead[i + 1] = leading(*states)
        trail[i + 1] = trailing(*states)
        start[i + 1] = states[0]

    @pl.loop(0, 8)
    def _(i):
        cubes = cubics(nodes, i)
        m = mob[i]
        r = rea[i]
        v1[i] = nodes[0, i] + m * laplace(lead[i + 1], lead[i], lead[i + 2]) + r * leading(*cubes)
        step[i] = m * laplace(trail[i + 1], trail[i], trail[i + 2]) + r * trailing(*cubes)
        first[i] = m * laplace(start[i + 1], start[i], start[i + 2]) + r * cubes[0]


def reduced(mix):
    half = mix.shape[0] // 2
    even = mix[pl.ds(0, half, stride=2), :]
    odd = mix[pl.ds(1, half, stride=2), :]
    return 0.5 * even + 0.25 * (odd + roll(odd, 1, 0))


def widen(d, wide, j):
    half = d.shape[0]
    wide[j, pl.ds(0, half, stride=2), :] = d
    wide[j, pl.ds(1, half, stride=2), :] = 0.5 * (d + roll(d, -1, 0))


def half_force(mid, low, high, mob, rea):
    planar = low + high + roll(mid, 1, 0) + roll(mid, -1, 0)
    vertical = roll(mid, 1, 1) + roll(mid, -1, 1)
    return mob * (planar + 4.0 * vertical - 12.0 * mid) + rea * cubic(mid)


def fine_kernel(
    nodes, mob, rea, left, right, to_right, to_left, own, v1_own, step_own, first_own,
    b1, b2, q, start, coarse, share, outer, rightward, leftward,
    mw, rw, v1, v2, step, first, f1, jj, mix,
):
    half = mob.shape[1] // 2

    @pl.loop(0, 8)
    def _(i):
        mw[i + 1] = mob[i]
        rw[i + 1] = rea[i]
        v1[i + 2] = v1_own[i]
        step[i + 1] = step_own[i]
        first[i] = first_own[i]

    for got, sent, place, far_place, beyond, plane in ((left, to_left, 1, 0, 0, 0), (right, to_right, 10, 11, 9, 7)):
        mw[beyond] = got[6]
        rw[beyond] = got[7]
        v1[far_place] = got[0]
        v1[place] = got[1] + got[6] * sent[4]
        step[beyond] = got[2] + got[6] * sent[5]
        v1[plane + 2] = v1_own[plane] + mob[plane] * got[4]
        step[plane + 1] = step_own[plane] + mob[plane] * got[5]
        first[plane] = first_own[plane] + mob[plane] * got[3]

    @pl.loop(0, 10, unroll=2)
    def _(i):
        a = v1[i + 1]
        force = mw[i] * laplace(a, v1[i], v1[i + 2]) + rw[i] * cubic(a)
        f1[i] = force
        v2[i] = a + (substep * force + step[i])

    @pl.loop(0, 8, unroll=2)
    def _(i):
        a = v2[i + 1]
        force = mob[i] * laplace(a, v2[i], v2[i + 2]) + rea[i] * cubic(a)
        second = middle * f1[i + 1]
        jj[0, i] = edge * first[i] + second + far * force
        jj[1, i] = far * first[i] + second + edge * force

    for j in range(4):
        before = nodes[0, 2 * j - 1] if j > 0 else left[3]
        mix[0] = 0.5 * nodes[0, 2 * j] + 0.25 * (nodes[0, 2 * j + 1] + before)
        mix[1] = 0.5 * v1[2 * j + 2] + 0.25 * (v1[2 * j + 3] + v1[2 * j + 1])
        mix[2] = 0.5 * v2[2 * j + 1] + 0.25 * (v2[2 * j + 2] + v2[2 * j])
        for m in range(2):
            mix[3 + m] = 0.5 * jj[m, 2 * j] + 0.25 * jj[m, 2 * j + 1]
            if j > 0:
                mix[3 + m] = mix[3 + m] + 0.25 * jj[m, 2 * j - 1]
        start[j] = reduced(mix.at[0])
        for m in range(2):
            coarse[m, j] = reduced(mix.at[1 + m])
            q[4 * m + j] = reduced(mix.at[3 + m])
    mix[0] = nodes[0, 7]
    start[4] = right[9, pl.ds(half, half), :] + 0.25 * reduced(mix.at[0])
    for m in range(2):
        mix[1 + m] = jj[m, 7]
        share[m] = 0.25 * reduced(mix.at[1 + m])

    outer[0] = 0.125 * right[6, pl.ds(0, half, stride=2), :]
    outer[1] = 0.5 * right[7, pl.ds(0, half, stride=2), :]
    for j in range(3):
        for side, got in enumerate((left, right)):
            outer[2 + 3 * side + j] = got[8 + j // 2, pl.ds(j % 2 * half, half), :]

    empty = jnp.zeros_like(share[0])
    for j in range(4):
        low = start[j - 1] if j > 0 else empty
        q[j] = q[j] - half_force(start[j], low, start[j + 1], own[0, j], own[1, j])
        low = coarse[0, j - 1] if j > 0 else empty
        high = coarse[0, j + 1] if j < 3 else empty
        q[4 + j] = q[4 + j] - half_force(coarse[0, j], low, high, own[0, j], own[1, j])

    for i in range(3):
        rightward[i] = q[1 + i]
        leftward[4 + i] = q[4 + i]
    for i in range(2):
        rightward[3 + i] = q[6 + i]
        rightward[10 + i] = share[i]
        leftward[11 + i] = coarse[i, 0]
    rightward[9] = coarse[0, 3]
    for i in range(4):
        rightward[5 + i] = start[i]
        leftward[i] = q[i]
        leftward[7 + i] = start[1 + i]

    for m, v, shift, b in ((0, v1, 2, b1), (1, v2, 1, b2)):
        for j in range(4):
            widen(coarse[m, j], mix, j)
        mix[4] = jnp.zeros_like(mix[4])
        for j in range(4):
            low = mix[j]
            b[2 * j] = v[2 * j + shift] - low
            b[2 * j + 1] = v[2 * j + 1 + shift] - 0.5 * (low + mix[j + 1])


def pack_kernel(q, start, c1, share, own, outer, from_left, from_right, window):
    window[0] = from_left[0]
    window[1] = from_left[1]
    window[2] = from_left[2]
    window[3] = q[0] + from_left[10] - own[0, 0] * from_left[8]
    for i in range(1, 4):
        window[3 + i] = q[i]
        window[7 + i] = from_right[i]
    window[7] = from_right[0] + share[0] - outer[0] * start[3]
    window[11] = from_left[3]
    window[12] = from_left[4]
    window[13] = q[4] + from_left[11] - own[0, 0] * from_left[9]
    window[14] = q[5]
    window[15] = q[6]
    window[16] = q[7] - own[0, 3] * from_right[11]
    window[17] = from_right[4] + share[1] - outer[0] * c1[3]
    window[18] = from_right[5]
    window[19] = from_right[6]
    for i in range(4):
        window[20 + i] = from_left[5 + i]
        window[29 + i] = from_right[7 + i]
    for i in range(5):
        window[24 + i] = start[i]
    for i in range(2):
        window[33 + i] = from_right[11 + i]
    for i in range(6):
        window[35 + i] = outer[2 + i]
    window[41] = c1[0]


def order(first, second, own, outer, out, mw, rw):
    for k, (source, coefficient) in enumerate(((first, mw), (second, rw))):
        for i in range(3):
            coefficient[i] = source[35 + i]
            coefficient[8 + i] = source[38 + i]
        for i in range(4):
            coefficient[3 + i] = own[k, i]
        coefficient[7] = outer[k]
    for i in range(20):
        out[i] = first[i]
    out[12] = first[12] - mw[2] * first[41]
    for i in range(7):
        out[20 + i] = second[2 + i]
    for i in range(5):
        out[27 + i] = second[13 + i]
    for i in range(2):
        out[32 + i] = first[33 + i]
        out[34 + i] = second[33 + i]
    for i in range(13):
        out[36 + i] = first[20 + i]


def sweep(x0, q, mw, rw, last, levels, x1, x2, x3):
    def level(source, target, count, terms, shift):
        for i in range(count):
            mid = source[i + 1]
            force = half_force(mid, source[i], source[i + 2], mw[i + shift], rw[i + shift])
            target[i] = mid + force + q[terms + i]

    level(x0, x1, 11, 0, 0)
    level(x1, x2, 9, 11, 1)
    level(x2, x3, 7, 20, 2)
    level(x3, last, 5, 27, 3)
    if last.shape[0] > 5:
        last[5] = q[35]
    if levels is not None:
        for i in range(4):
            levels[0, i] = x0[i + 4]
            levels[1, i] = x1[i + 3]
            levels[2, i] = x2[i + 2]
            levels[3, i] = x3[i + 1]
            levels[4, i] = last[i]
        levels[1, 4] = x1[7] - q[32]
        levels[2, 4] = x2[6] - q[33]
        levels[3, 4] = x3[5] - q[34]
        levels[4, 4] = last[4] - q[35]


def first_kernel(flags, mine, other, own, outer, last, ordered, mw, rw, x1, x2, x3):
    pl.when(flags[0] == 0)(lambda: order(mine, other, own, outer, ordered, mw, rw))
    pl.when(flags[0] != 0)(lambda: order(other, mine, own, outer, ordered, mw, rw))
    sweep(ordered.at[pl.ds(36, 13)], ordered, mw, rw, last, None, x1, x2, x3)


def turn_kernel(final, flags, ordered, mw, rw, mid, low, high, last, *refs):
    levels = refs[0] if final else None
    x0, x1, x2, x3 = refs[-4:]

    @pl.when(flags[1] == 0)
    def _():
        for i in range(13):
            x0[i] = ordered[36 + i]

    @pl.when(flags[1] != 0)
    def _():
        for i in range(4):
            x0[i] = low[i]
            x0[9 + i] = high[i]
        for i in range(5):
            x0[4 + i] = mid[i]

    sweep(x0, ordered, mw, rw, last, levels, x1, x2, x3)
    if final:
        levels[0, 4] = mid[4] - mid[5]


def final_kernel(flags, start, b1, b2, b_before, levels, out, wide):
    core = flags[0]
    for m, b in ((0, b_before), (1, b1), (2, b2)):

        def corrected(m=m, b=b):
            for j in range(5):
                widen(levels[2 * core + m, j], wide, j)
            for j in range(4):
                low = wide[j]
                out[0, m, 2 * j] = b[2 * j] + low
                out[0, m, 2 * j + 1] = b[2 * j + 1] + 0.5 * (low + wide[j + 1])

        if m == 0:
            pl.when(flags[2] != 0)(corrected)

            @pl.when(flags[2] == 0)
            def _():
                for i in range(8):
                    out[0, 0, i] = start[i]

        else:
            corrected()


def body(nodes, mobility, reaction):
    states = nodes[0]
    _, blocks, ny, nz = states.shape
    hy = ny // 2
    plane = (ny, nz)
    small = (hy, nz)
    slice_index = lax.axis_index("tm")
    flags = jnp.stack([slice_index % 2, slice_index // 2, slice_index]).astype(jnp.int32)

    own, to_right, to_left = pl.pallas_call(
        edge_kernel,
        out_shape=[jax.ShapeDtypeStruct(s, jnp.float32) for s in ((2, 4) + small, (10,) + plane, (10,) + plane)],
        in_specs=[pl.BlockSpec(memory_space=pltpu.SMEM)] + [pl.BlockSpec(memory_space=pltpu.HBM)] * 3,
        out_specs=[pl.BlockSpec(memory_space=pltpu.VMEM)] * 3,
        scratch_shapes=[pltpu.VMEM(s, jnp.float32) for s in (plane, (3, 8) + plane, (8,) + plane, (8,) + plane)]
        + [pltpu.SemaphoreType.DMA((8,))],
        compiler_params=pltpu.CompilerParams(vmem_limit_bytes=8 * 1024 * 1024),
        cost_estimate=cost(10**6, 4 * 10**6),
    )(flags, *(pltpu.with_memory_space_constraint(a, pltpu.HBM) for a in (states, mobility, reaction)))
    left = ring(to_right, "space", 1)
    right = ring(to_left, "space", -1)
    v1, step, first = call(
        local_kernel, [(8,) + plane] * 3, [(10,) + plane] * 3, states, mobility, reaction, flops=10**7
    )
    b1, b2, q, start, coarse, share, outer, to_right, to_left = call(
        fine_kernel,
        [(8,) + plane, (8,) + plane, (8,) + small, (5,) + small, (2, 4) + small, (2,) + small, (8,) + small, (12,) + small,
         (13,) + small],
        [(10,) + plane, (10,) + plane, (12,) + plane, (10,) + plane, (10,) + plane, (8,) + plane, (10,) + plane,
         (2, 8) + plane, (5,) + plane],
        states, mobility, reaction, left, right, to_right, to_left, own, v1, step, first, flops=2 * 10**7, limit=16,
    )
    q_left = ring(to_right, "space", 1)
    q_right = ring(to_left, "space", -1)
    b_before = ring(b2, "tm", 1)
    (mine,) = call(pack_kernel, [(42,) + small], [], q, start, coarse[0], share, own, outer, q_left, q_right)
    other = swapped(mine)
    levels_shape = [(11,) + small, (9,) + small, (7,) + small]
    last, ordered, mw, rw = call(
        first_kernel, [(5,) + small, (49,) + small, (11,) + small, (11,) + small], levels_shape,
        flags, mine, other, own, outer, scalars=1,
    )
    turns = lax.axis_size("tm") // 2
    for turn in range(1, turns):
        final = turn == turns - 1
        mid = ring(last, "tm", 2)
        low = ring(mid[0:4], "space", 1)
        high = ring(mid[1:5], "space", -1)
        if turn == 1:
            low, high, b_before = together(low, high, b_before)
        last, *levels = call(
            functools.partial(turn_kernel, final), [(6 if turn == turns - 2 else 5,) + small] + [(5, 5) + small] * final, [(13,) + small] + levels_shape,
            flags, ordered, mw, rw, mid, low, high, scalars=1,
        )
    (out,) = call(
        final_kernel, [(1, 3, 8) + plane], [(5,) + plane], flags, states[0], b1, b2, b_before, levels[0], scalars=1,
    )
    return out


def solution(mesh):
    return jax.shard_map(
        body,
        mesh=mesh,
        in_specs=(
            P("tm", None, "space", None, None),
            P("space", None, None),
            P("space", None, None),
        ),
        out_specs=P("tm", None, "space", None, None),
        check_vma=False,
    )
```

```python
import functools
import jax
import jax.numpy as jnp
from jax import lax
from jax.experimental import pallas as pl
from jax.experimental.pallas import tpu as pltpu
from jax.sharding import PartitionSpec as P

edge = 5.0 / 24.0
middle = 1.0 / 3.0
far = -1.0 / 24.0
substep = 0.5


def roll(values, amount, axis):
    return pltpu.roll(values, amount % values.shape[axis], axis)


def around(values):
    return roll(values, 1, 0) + roll(values, -1, 0) + roll(values, 1, 1) + roll(values, -1, 1)


def cubic(values):
    return values - values * values * values


def cost(flops, moved):
    return pl.CostEstimate(flops=flops, bytes_accessed=moved, transcendentals=0)


def ring(values, axis, distance):
    count = lax.axis_size(axis)
    return lax.ppermute(values, axis, [(i, (i + distance) % count) for i in range(count)])


def together(*values):
    return lax.optimization_barrier(values)


def hop(values, turn):
    return lax.ppermute(values, "tm", [(2 * turn - 2 + core, 2 * turn + core) for core in range(2)])


def swapped(values):
    count = lax.axis_size("tm")
    return lax.ppermute(values, "tm", [(i, i ^ 1) for i in range(count)])


def call(kernel, outs, scratch, *args, flops=10**6, scalars=0, limit=8):
    moved = sum(a.size * 4 for a in args) + sum(4 * functools.reduce(lambda x, y: x * y, s) for s in outs)
    result = pl.pallas_call(
        kernel,
        out_shape=[jax.ShapeDtypeStruct(s, jnp.float32) for s in outs],
        in_specs=[pl.BlockSpec(memory_space=pltpu.SMEM)] * scalars
        + [pl.BlockSpec(memory_space=pltpu.VMEM)] * (len(args) - scalars),
        out_specs=[pl.BlockSpec(memory_space=pltpu.VMEM) for _ in outs],
        scratch_shapes=[pltpu.VMEM(s, jnp.float32) for s in scratch],
        compiler_params=pltpu.CompilerParams(vmem_limit_bytes=limit * 1024 * 1024),
        cost_estimate=cost(flops, moved),
    )(*args)
    return result


def laplace(mid, *beside):
    total = around(mid) - 6.0 * mid
    for values in beside:
        total = total + values
    return total


def leading(x0, x1, x2):
    return edge * x0 + middle * x1 + far * x2


def trailing(x0, x1, x2):
    return far * x0 + (middle - substep) * x1 + edge * x2


def cubics(nodes, plane):
    return [cubic(nodes[m, plane]) for m in range(3)]


def edge_kernel(flags, nodes_hbm, mob_hbm, rea_hbm, own, rightward, leftward, mix, nodes, mob, rea, sems):
    half = mob.shape[1] // 2
    copies = [pltpu.make_async_copy(mob_hbm, mob, sems.at[0]), pltpu.make_async_copy(rea_hbm, rea, sems.at[1])]
    for m in range(3):
        for k, first in enumerate((5, 0)):
            part = pl.ds(first, 3)
            copies.append(pltpu.make_async_copy(nodes_hbm.at[m, part], nodes.at[m, part], sems.at[2 + 2 * m + k]))
    for copy in copies:
        copy.start()
    for copy in copies[:2]:
        copy.wait()
    for k, (source, scale) in enumerate(((mob, 0.125), (rea, 0.5))):
        for j in range(4):
            own[k, j] = scale * source[2 * j, pl.ds(0, half, stride=2), :]

    for core in range(2):

        @pl.when(flags[0] == core)
        def _():
            for j in range(3):
                for out in (rightward, leftward):
                    out[8 + j // 2, pl.ds(j % 2 * half, half), :] = own[core, j + 1]

    for copy in copies[2:]:
        copy.wait()

    for out, outer, inner, third in ((rightward, 7, 6, 5), (leftward, 0, 1, 2)):
        lead = [leading(nodes[0, p], nodes[1, p], nodes[2, p]) for p in (outer, inner, third)]
        cubes = cubics(nodes, inner)
        out[0] = nodes[0, inner] + mob[inner] * laplace(lead[1], lead[0], lead[2]) + rea[inner] * leading(*cubes)
        cubes = cubics(nodes, outer)
        out[1] = nodes[0, outer] + mob[outer] * laplace(lead[0], lead[1]) + rea[outer] * leading(*cubes)
        out[4] = lead[0]
        trail = [trailing(nodes[0, p], nodes[1, p], nodes[2, p]) for p in (outer, inner)]
        out[2] = mob[outer] * laplace(trail[0], trail[1]) + rea[outer] * trailing(*cubes)
        out[5] = trail[0]
        out[3] = nodes[0, outer]
        out[6] = mob[outer]
        out[7] = rea[outer]
    mix[...] = 0.5 * nodes[0, 0] + 0.25 * nodes[0, 1]
    leftward[9, pl.ds(half, half), :] = reduced(mix)
    rightward[9, pl.ds(half, half), :] = jnp.zeros_like(own[0, 0])


def local_kernel(nodes, mob, rea, v1, step, first, lead, trail, start):
    for array in (lead, trail, start):
        for i in (0, 9):
            array[i] = jnp.zeros_like(array[i])

    @pl.loop(0, 8)
    def _(i):
        states = nodes[0, i], nodes[1, i], nodes[2, i]
        lead[i + 1] = leading(*states)
        trail[i + 1] = trailing(*states)
        start[i + 1] = states[0]

    @pl.loop(0, 8)
    def _(i):
        cubes = cubics(nodes, i)
        m = mob[i]
        r = rea[i]
        v1[i] = nodes[0, i] + m * laplace(lead[i + 1], lead[i], lead[i + 2]) + r * leading(*cubes)
        step[i] = m * laplace(trail[i + 1], trail[i], trail[i + 2]) + r * trailing(*cubes)
        first[i] = m * laplace(start[i + 1], start[i], start[i + 2]) + r * cubes[0]


def reduced(mix):
    half = mix.shape[0] // 2
    even = mix[pl.ds(0, half, stride=2), :]
    odd = mix[pl.ds(1, half, stride=2), :]
    return 0.5 * even + 0.25 * (odd + roll(odd, 1, 0))


def widen(d, wide, j):
    half = d.shape[0]
    wide[j, pl.ds(0, half, stride=2), :] = d
    wide[j, pl.ds(1, half, stride=2), :] = 0.5 * (d + roll(d, -1, 0))


def half_force(mid, low, high, mob, rea):
    planar = low + high + roll(mid, 1, 0) + roll(mid, -1, 0)
    vertical = roll(mid, 1, 1) + roll(mid, -1, 1)
    return mob * (planar + 4.0 * vertical - 12.0 * mid) + rea * cubic(mid)


def fine_kernel(
    flags, nodes, mob, rea, left, right, to_right, to_left, own, v1_own, step_own, first_own,
    v1_out, v2_out, q, start, coarse, share, outer, rightward, leftward,
    mw, rw, v1, v2, step, first, f1, jj, mix,
):
    half = mob.shape[1] // 2

    @pl.loop(0, 8)
    def _(i):
        mw[i + 1] = mob[i]
        rw[i + 1] = rea[i]
        v1[i + 2] = v1_own[i]
        step[i + 1] = step_own[i]
        first[i] = first_own[i]

    for got, sent, place, far_place, beyond, plane in ((left, to_left, 1, 0, 0, 0), (right, to_right, 10, 11, 9, 7)):
        mw[beyond] = got[6]
        rw[beyond] = got[7]
        v1[far_place] = got[0]
        v1[place] = got[1] + got[6] * sent[4]
        step[beyond] = got[2] + got[6] * sent[5]
        v1[plane + 2] = v1_own[plane] + mob[plane] * got[4]
        step[plane + 1] = step_own[plane] + mob[plane] * got[5]
        first[plane] = first_own[plane] + mob[plane] * got[3]

    @pl.loop(0, 10, unroll=2)
    def _(i):
        a = v1[i + 1]
        force = mw[i] * laplace(a, v1[i], v1[i + 2]) + rw[i] * cubic(a)
        f1[i] = force
        v2[i] = a + (substep * force + step[i])

    @pl.loop(0, 8, unroll=2)
    def _(i):
        a = v2[i + 1]
        force = mob[i] * laplace(a, v2[i], v2[i + 2]) + rea[i] * cubic(a)
        second = middle * f1[i + 1]
        v1_out[i] = v1[i + 2]
        v2_out[i] = a
        jj[0, i] = edge * first[i] + second + far * force
        jj[1, i] = far * first[i] + second + edge * force

    for j in range(4):
        before = nodes[0, 2 * j - 1] if j > 0 else left[3]
        mix[0] = 0.5 * nodes[0, 2 * j] + 0.25 * (nodes[0, 2 * j + 1] + before)
        mix[1] = 0.5 * v1[2 * j + 2] + 0.25 * (v1[2 * j + 3] + v1[2 * j + 1])
        mix[2] = 0.5 * v2[2 * j + 1] + 0.25 * (v2[2 * j + 2] + v2[2 * j])
        for m in range(2):
            mix[3 + m] = 0.5 * jj[m, 2 * j] + 0.25 * jj[m, 2 * j + 1]
            if j > 0:
                mix[3 + m] = mix[3 + m] + 0.25 * jj[m, 2 * j - 1]
        start[j] = reduced(mix.at[0])
        for m in range(2):
            coarse[m, j] = reduced(mix.at[1 + m])
            q[4 * m + j] = reduced(mix.at[3 + m])
    mix[0] = nodes[0, 7]
    start[4] = right[9, pl.ds(half, half), :] + 0.25 * reduced(mix.at[0])
    for m in range(2):
        mix[1 + m] = jj[m, 7]
        share[m] = 0.25 * reduced(mix.at[1 + m])

    outer[0] = 0.125 * right[6, pl.ds(0, half, stride=2), :]
    outer[1] = 0.5 * right[7, pl.ds(0, half, stride=2), :]
    for j in range(3):
        for side, got in enumerate((left, right)):
            outer[2 + 3 * side + j] = got[8 + j // 2, pl.ds(j % 2 * half, half), :]

    empty = jnp.zeros_like(share[0])

    @pl.when(flags[2] == 0)
    def _():
        for j in range(4):
            q[j] = q[j] + start[j]

    @pl.when(flags[2] != 0)
    def _():
        for j in range(4):
            low = start[j - 1] if j > 0 else empty
            q[j] = q[j] - half_force(start[j], low, start[j + 1], own[0, j], own[1, j])

    for j in range(4):
        low = coarse[0, j - 1] if j > 0 else empty
        high = coarse[0, j + 1] if j < 3 else empty
        q[4 + j] = q[4 + j] - half_force(coarse[0, j], low, high, own[0, j], own[1, j])

    for i in range(3):
        rightward[i] = q[1 + i]
        leftward[4 + i] = q[4 + i]
    for i in range(2):
        rightward[3 + i] = q[6 + i]
        rightward[7 + i] = share[i]
        leftward[7 + i] = coarse[i, 0]
    rightward[5] = start[3]
    rightward[6] = coarse[0, 3]
    for i in range(4):
        leftward[i] = q[i]


def base_kernel(v1, v2, coarse, from_left, from_right, b1, b2, mix):
    del from_left
    for m, v, b in ((0, v1, b1), (1, v2, b2)):
        for j in range(4):
            widen(coarse[m, j], mix, j)
        widen(from_right[7 + m], mix, 4)
        for j in range(4):
            low = mix[j]
            b[2 * j] = v[2 * j] - low
            b[2 * j + 1] = v[2 * j + 1] - 0.5 * (low + mix[j + 1])


def pack_kernel(flags, q, start, c1, share, own, outer, from_left, from_right, window):
    keep = jnp.where(flags[2] == 0, 0.0, 1.0)
    window[0] = from_left[0]
    window[1] = from_left[1]
    window[2] = from_left[2]
    window[3] = q[0] + from_left[7] - keep * own[0, 0] * from_left[5]
    for i in range(1, 4):
        window[3 + i] = q[i]
        window[7 + i] = from_right[i]
    window[7] = from_right[0] + share[0] - keep * outer[0] * start[3]
    window[11] = from_left[3]
    window[12] = from_left[4]
    window[13] = q[4] + from_left[8] - own[0, 0] * from_left[6]
    window[14] = q[5]
    window[15] = q[6]
    window[16] = q[7] - own[0, 3] * from_right[7]
    window[17] = from_right[4] + share[1] - outer[0] * c1[3]
    window[18] = from_right[5]
    window[19] = from_right[6]
    for i in range(6):
        window[20 + i] = outer[2 + i]
    window[26] = c1[0]


def order(first, second, own, outer, out, mw, rw):
    for k, (source, coefficient) in enumerate(((first, mw), (second, rw))):
        for i in range(3):
            coefficient[i] = source[20 + i]
            coefficient[8 + i] = source[23 + i]
        for i in range(4):
            coefficient[3 + i] = own[k, i]
        coefficient[7] = outer[k]
    for i in range(20):
        out[i] = first[i]
    out[12] = first[12] - mw[2] * first[26]
    for i in range(7):
        out[20 + i] = second[2 + i]
    for i in range(5):
        out[27 + i] = second[13 + i]


def sweep(x0, q, mw, rw, last, levels, x1, x2, x3):
    def level(source, target, count, terms, shift):
        for i in range(count):
            mid = source[i + 1]
            force = half_force(mid, source[i], source[i + 2], mw[i + shift], rw[i + shift])
            target[i] = mid + force + q[terms + i]

    if x0 is not None:
        level(x0, x1, 11, 0, 0)
    level(x1, x2, 9, 11, 1)
    level(x2, x3, 7, 20, 2)
    level(x3, last, 5, 27, 3)
    if levels is not None:
        for i in range(5):
            levels[0, i] = x0[i + 4]
            levels[1, i] = x1[i + 3]
            levels[2, i] = x2[i + 2]
            levels[3, i] = x3[i + 1]
            levels[4, i] = last[i]


def first_kernel(flags, mine, other, own, outer, last, ordered, mw, rw, x2, x3):
    pl.when(flags[0] == 0)(lambda: order(mine, other, own, outer, ordered, mw, rw))
    pl.when(flags[0] != 0)(lambda: order(other, mine, own, outer, ordered, mw, rw))
    sweep(None, ordered, mw, rw, last, None, ordered.at[pl.ds(0, 11)], x2, x3)


def turn_kernel(turn, final, flags, ordered, mw, rw, mid, low, high, *refs):
    if turn > 1:
        kept, *refs = refs
    last, x0 = refs[:2]
    levels = refs[2] if final else None
    x1, x2, x3 = refs[-3:]

    @pl.when(flags[1] != turn)
    def _():
        for i in range(13):
            x0[i] = kept[i] if turn > 1 else jnp.zeros_like(x0[i])

    @pl.when(flags[1] == turn)
    def _():
        for i in range(4):
            x0[i] = low[i]
            x0[9 + i] = high[i]
        for i in range(5):
            x0[4 + i] = mid[i]

    sweep(x0, ordered, mw, rw, last, levels, x1, x2, x3)


def final_kernel(flags, start, b1, b2, b_before, levels, out, wide):
    core = flags[0]
    for m, b in ((0, b_before), (1, b1), (2, b2)):

        def corrected(m=m, b=b):
            for j in range(5):
                widen(levels[2 * core + m, j], wide, j)
            for j in range(4):
                low = wide[j]
                out[0, m, 2 * j] = b[2 * j] + low
                out[0, m, 2 * j + 1] = b[2 * j + 1] + 0.5 * (low + wide[j + 1])

        if m == 0:
            pl.when(flags[2] != 0)(corrected)

            @pl.when(flags[2] == 0)
            def _():
                for i in range(8):
                    out[0, 0, i] = start[i]

        else:
            corrected()


def body(nodes, mobility, reaction):
    states = nodes[0]
    _, blocks, ny, nz = states.shape
    hy = ny // 2
    plane = (ny, nz)
    small = (hy, nz)
    slice_index = lax.axis_index("tm")
    flags = jnp.stack([slice_index % 2, slice_index // 2, slice_index]).astype(jnp.int32)

    own, to_right, to_left = pl.pallas_call(
        edge_kernel,
        out_shape=[jax.ShapeDtypeStruct(s, jnp.float32) for s in ((2, 4) + small, (10,) + plane, (10,) + plane)],
        in_specs=[pl.BlockSpec(memory_space=pltpu.SMEM)] + [pl.BlockSpec(memory_space=pltpu.HBM)] * 3,
        out_specs=[pl.BlockSpec(memory_space=pltpu.VMEM)] * 3,
        scratch_shapes=[pltpu.VMEM(s, jnp.float32) for s in (plane, (3, 8) + plane, (8,) + plane, (8,) + plane)]
        + [pltpu.SemaphoreType.DMA((8,))],
        compiler_params=pltpu.CompilerParams(vmem_limit_bytes=8 * 1024 * 1024),
        cost_estimate=cost(10**6, 4 * 10**6),
    )(flags, *(pltpu.with_memory_space_constraint(a, pltpu.HBM) for a in (states, mobility, reaction)))
    left = ring(to_right, "space", 1)
    right = ring(to_left, "space", -1)
    v1, step, first = call(
        local_kernel, [(8,) + plane] * 3, [(10,) + plane] * 3, states, mobility, reaction, flops=10**7
    )
    v1, v2, q, start, coarse, share, outer, to_right, to_left = call(
        fine_kernel,
        [(8,) + plane, (8,) + plane, (8,) + small, (5,) + small, (2, 4) + small, (2,) + small, (8,) + small, (9,) + small,
         (9,) + small],
        [(10,) + plane, (10,) + plane, (12,) + plane, (10,) + plane, (10,) + plane, (8,) + plane, (10,) + plane,
         (2, 8) + plane, (5,) + plane],
        flags, states, mobility, reaction, left, right, to_right, to_left, own, v1, step, first,
        flops=2 * 10**7, limit=16, scalars=1,
    )
    q_left = ring(to_right, "space", 1)
    q_right = ring(to_left, "space", -1)
    b1, b2 = call(base_kernel, [(8,) + plane, (8,) + plane], [(5,) + plane], v1, v2, coarse, q_left, q_right)
    b_before = ring(b2, "tm", 1)
    (mine,) = call(
        pack_kernel, [(27,) + small], [], flags, q, start, coarse[0], share, own, outer, q_left, q_right, scalars=1
    )
    other = swapped(mine)
    levels_shape = [(11,) + small, (9,) + small, (7,) + small]
    last, ordered, mw, rw = call(
        first_kernel, [(5,) + small, (32,) + small, (11,) + small, (11,) + small], levels_shape[1:],
        flags, mine, other, own, outer, scalars=1,
    )
    turns = lax.axis_size("tm") // 2
    for turn in range(1, turns):
        final = turn == turns - 1
        mid = hop(last, turn)
        low = ring(mid[0:4], "space", 1)
        high = ring(mid[1:5], "space", -1)
        if turn == 1:
            low, high, b_before = together(low, high, b_before)
        last, kept, *levels = call(
            functools.partial(turn_kernel, turn, final),
            [(5,) + small, (13,) + small] + [(5, 5) + small] * final,
            levels_shape,
            flags, ordered, mw, rw, mid, low, high, *([kept] if turn > 1 else []), scalars=1,
        )
    (out,) = call(
        final_kernel, [(1, 3, 8) + plane], [(5,) + plane], flags, states[0], b1, b2, b_before, levels[0], scalars=1,
    )
    return out


def solution(mesh):
    return jax.shard_map(
        body,
        mesh=mesh,
        in_specs=(
            P("tm", None, "space", None, None),
            P("space", None, None),
            P("space", None, None),
        ),
        out_specs=P("tm", None, "space", None, None),
        check_vma=False,
    )
```

```python
import functools
import jax
import jax.numpy as jnp
from jax import lax
from jax.experimental import pallas as pl
from jax.experimental.pallas import tpu as pltpu
from jax.sharding import PartitionSpec as P

edge = 5.0 / 24.0
middle = 1.0 / 3.0
far = -1.0 / 24.0
substep = 0.5


def roll(values, amount, axis):
    return pltpu.roll(values, amount % values.shape[axis], axis)


def around(values):
    return roll(values, 1, 0) + roll(values, -1, 0) + roll(values, 1, 1) + roll(values, -1, 1)


def cubic(values):
    return values - values * values * values


def cost(flops, moved):
    return pl.CostEstimate(flops=flops, bytes_accessed=moved, transcendentals=0)


def ring(values, axis, distance):
    count = lax.axis_size(axis)
    return lax.ppermute(values, axis, [(i, (i + distance) % count) for i in range(count)])


def together(*values):
    return lax.optimization_barrier(values)


def hop(values, turn):
    return lax.ppermute(values, "tm", [(2 * turn - 2 + core, 2 * turn + core) for core in range(2)])


def swapped(values):
    count = lax.axis_size("tm")
    return lax.ppermute(values, "tm", [(i, i ^ 1) for i in range(count)])


def call(kernel, outs, scratch, *args, flops=10**6, scalars=0, limit=8):
    moved = sum(a.size * 4 for a in args) + sum(4 * functools.reduce(lambda x, y: x * y, s) for s in outs)
    result = pl.pallas_call(
        kernel,
        out_shape=[jax.ShapeDtypeStruct(s, jnp.float32) for s in outs],
        in_specs=[pl.BlockSpec(memory_space=pltpu.SMEM)] * scalars
        + [pl.BlockSpec(memory_space=pltpu.VMEM)] * (len(args) - scalars),
        out_specs=[pl.BlockSpec(memory_space=pltpu.VMEM) for _ in outs],
        scratch_shapes=[pltpu.VMEM(s, jnp.float32) for s in scratch],
        compiler_params=pltpu.CompilerParams(vmem_limit_bytes=limit * 1024 * 1024),
        cost_estimate=cost(flops, moved),
    )(*args)
    return result


def laplace(mid, *beside):
    total = around(mid) - 6.0 * mid
    for values in beside:
        total = total + values
    return total


def leading(x0, x1, x2):
    return edge * x0 + middle * x1 + far * x2


def trailing(x0, x1, x2):
    return far * x0 + (middle - substep) * x1 + edge * x2


def cubics(nodes, plane):
    return [cubic(nodes[m, plane]) for m in range(3)]


def edge_kernel(flags, nodes_hbm, mob_hbm, rea_hbm, own, rightward, leftward, mix, nodes, mob, rea, sems):
    half = mob.shape[1] // 2
    copies = [pltpu.make_async_copy(mob_hbm, mob, sems.at[0]), pltpu.make_async_copy(rea_hbm, rea, sems.at[1])]
    for m in range(3):
        for k, first in enumerate((5, 0)):
            part = pl.ds(first, 3)
            copies.append(pltpu.make_async_copy(nodes_hbm.at[m, part], nodes.at[m, part], sems.at[2 + 2 * m + k]))
    for copy in copies:
        copy.start()
    for copy in copies[:2]:
        copy.wait()
    for k, (source, scale) in enumerate(((mob, 0.125), (rea, 0.5))):
        for j in range(4):
            own[k, j] = scale * source[2 * j, pl.ds(0, half, stride=2), :]

    for core in range(2):

        @pl.when(flags[0] == core)
        def _():
            for j in range(3):
                for out in (rightward, leftward):
                    out[8 + j // 2, pl.ds(j % 2 * half, half), :] = own[core, j + 1]

    for copy in copies[2:]:
        copy.wait()

    for out, outer, inner, third in ((rightward, 7, 6, 5), (leftward, 0, 1, 2)):
        lead = [leading(nodes[0, p], nodes[1, p], nodes[2, p]) for p in (outer, inner, third)]
        cubes = cubics(nodes, inner)
        out[0] = nodes[0, inner] + mob[inner] * laplace(lead[1], lead[0], lead[2]) + rea[inner] * leading(*cubes)
        cubes = cubics(nodes, outer)
        out[1] = nodes[0, outer] + mob[outer] * laplace(lead[0], lead[1]) + rea[outer] * leading(*cubes)
        out[4] = lead[0]
        trail = [trailing(nodes[0, p], nodes[1, p], nodes[2, p]) for p in (outer, inner)]
        out[2] = mob[outer] * laplace(trail[0], trail[1]) + rea[outer] * trailing(*cubes)
        out[5] = trail[0]
        out[3] = nodes[0, outer]
        out[6] = mob[outer]
        out[7] = rea[outer]
    mix[...] = 0.5 * nodes[0, 0] + 0.25 * nodes[0, 1]
    leftward[9, pl.ds(half, half), :] = reduced(mix)
    rightward[9, pl.ds(half, half), :] = jnp.zeros_like(own[0, 0])


def local_kernel(nodes, mob, rea, v1, step, first, lead, trail, start):
    for array in (lead, trail, start):
        for i in (0, 9):
            array[i] = jnp.zeros_like(array[i])

    @pl.loop(0, 8)
    def _(i):
        states = nodes[0, i], nodes[1, i], nodes[2, i]
        lead[i + 1] = leading(*states)
        trail[i + 1] = trailing(*states)
        start[i + 1] = states[0]

    @pl.loop(0, 8)
    def _(i):
        cubes = cubics(nodes, i)
        m = mob[i]
        r = rea[i]
        v1[i] = nodes[0, i] + m * laplace(lead[i + 1], lead[i], lead[i + 2]) + r * leading(*cubes)
        step[i] = m * laplace(trail[i + 1], trail[i], trail[i + 2]) + r * trailing(*cubes)
        first[i] = m * laplace(start[i + 1], start[i], start[i + 2]) + r * cubes[0]


def reduced(mix):
    half = mix.shape[0] // 2
    even = mix[pl.ds(0, half, stride=2), :]
    odd = mix[pl.ds(1, half, stride=2), :]
    return 0.5 * even + 0.25 * (odd + roll(odd, 1, 0))


def widen(d, wide, j):
    half = d.shape[0]
    wide[j, pl.ds(0, half, stride=2), :] = d
    wide[j, pl.ds(1, half, stride=2), :] = 0.5 * (d + roll(d, -1, 0))


def half_force(mid, low, high, mob, rea):
    planar = low + high + roll(mid, 1, 0) + roll(mid, -1, 0)
    vertical = roll(mid, 1, 1) + roll(mid, -1, 1)
    return mob * (planar + 4.0 * vertical - 12.0 * mid) + rea * cubic(mid)


def fine_kernel(
    flags, nodes, mob, rea, left, right, to_right, to_left, own, v1_own, step_own, first_own,
    v1_out, v2_out, q, start, coarse, share, outer, rightward, leftward,
    mw, rw, v1, v2, step, first, f1, jj, mix,
):
    half = mob.shape[1] // 2

    @pl.loop(0, 8)
    def _(i):
        mw[i + 1] = mob[i]
        rw[i + 1] = rea[i]
        v1[i + 2] = v1_own[i]
        step[i + 1] = step_own[i]
        first[i] = first_own[i]

    for got, sent, place, far_place, beyond, plane in ((left, to_left, 1, 0, 0, 0), (right, to_right, 10, 11, 9, 7)):
        mw[beyond] = got[6]
        rw[beyond] = got[7]
        v1[far_place] = got[0]
        v1[place] = got[1] + got[6] * sent[4]
        step[beyond] = got[2] + got[6] * sent[5]
        v1[plane + 2] = v1_own[plane] + mob[plane] * got[4]
        step[plane + 1] = step_own[plane] + mob[plane] * got[5]
        first[plane] = first_own[plane] + mob[plane] * got[3]

    @pl.loop(0, 10, unroll=2)
    def _(i):
        a = v1[i + 1]
        force = mw[i] * laplace(a, v1[i], v1[i + 2]) + rw[i] * cubic(a)
        f1[i] = force
        v2[i] = a + (substep * force + step[i])

    @pl.loop(0, 8, unroll=2)
    def _(i):
        a = v2[i + 1]
        force = mob[i] * laplace(a, v2[i], v2[i + 2]) + rea[i] * cubic(a)
        second = middle * f1[i + 1]
        v1_out[i] = v1[i + 2]
        v2_out[i] = a
        jj[0, i] = edge * first[i] + second + far * force
        jj[1, i] = far * first[i] + second + edge * force

    for j in range(4):
        before = nodes[0, 2 * j - 1] if j > 0 else left[3]
        mix[0] = 0.5 * nodes[0, 2 * j] + 0.25 * (nodes[0, 2 * j + 1] + before)
        mix[1] = 0.5 * v1[2 * j + 2] + 0.25 * (v1[2 * j + 3] + v1[2 * j + 1])
        mix[2] = 0.5 * v2[2 * j + 1] + 0.25 * (v2[2 * j + 2] + v2[2 * j])
        for m in range(2):
            mix[3 + m] = 0.5 * jj[m, 2 * j] + 0.25 * jj[m, 2 * j + 1]
            if j > 0:
                mix[3 + m] = mix[3 + m] + 0.25 * jj[m, 2 * j - 1]
        start[j] = reduced(mix.at[0])
        for m in range(2):
            coarse[m, j] = reduced(mix.at[1 + m])
            q[4 * m + j] = reduced(mix.at[3 + m])
    mix[0] = nodes[0, 7]
    start[4] = right[9, pl.ds(half, half), :] + 0.25 * reduced(mix.at[0])
    for m in range(2):
        mix[1 + m] = jj[m, 7]
        share[m] = 0.25 * reduced(mix.at[1 + m])

    outer[0] = 0.125 * right[6, pl.ds(0, half, stride=2), :]
    outer[1] = 0.5 * right[7, pl.ds(0, half, stride=2), :]
    for j in range(3):
        for side, got in enumerate((left, right)):
            outer[2 + 3 * side + j] = got[8 + j // 2, pl.ds(j % 2 * half, half), :]

    empty = jnp.zeros_like(share[0])

    @pl.when(flags[2] == 0)
    def _():
        for j in range(4):
            q[j] = q[j] + start[j]

    @pl.when(flags[2] != 0)
    def _():
        for j in range(4):
            low = start[j - 1] if j > 0 else empty
            q[j] = q[j] - half_force(start[j], low, start[j + 1], own[0, j], own[1, j])

    for j in range(4):
        low = coarse[0, j - 1] if j > 0 else empty
        high = coarse[0, j + 1] if j < 3 else empty
        q[4 + j] = q[4 + j] - half_force(coarse[0, j], low, high, own[0, j], own[1, j])

    for i in range(3):
        rightward[i] = q[1 + i]
        leftward[4 + i] = q[4 + i]
    for i in range(2):
        rightward[3 + i] = q[6 + i]
        rightward[7 + i] = share[i]
        leftward[7 + i] = coarse[i, 0]
    rightward[5] = start[3]
    rightward[6] = coarse[0, 3]
    for i in range(4):
        leftward[i] = q[i]


def base_kernel(v1, v2, coarse, from_left, from_right, b1, b2, mix):
    del from_left
    for m, v, b in ((0, v1, b1), (1, v2, b2)):
        for j in range(4):
            widen(coarse[m, j], mix, j)
        widen(from_right[7 + m], mix, 4)
        for j in range(4):
            low = mix[j]
            b[2 * j] = v[2 * j] - low
            b[2 * j + 1] = v[2 * j + 1] - 0.5 * (low + mix[j + 1])


def pack_kernel(flags, q, start, c1, share, own, outer, from_left, from_right, window):
    keep = jnp.where(flags[2] == 0, 0.0, 1.0)
    window[0] = from_left[0]
    window[1] = from_left[1]
    window[2] = from_left[2]
    window[3] = q[0] + from_left[7] - keep * own[0, 0] * from_left[5]
    for i in range(1, 4):
        window[3 + i] = q[i]
        window[7 + i] = from_right[i]
    window[7] = from_right[0] + share[0] - keep * outer[0] * start[3]
    window[11] = from_left[3]
    window[12] = from_left[4]
    window[13] = q[4] + from_left[8] - own[0, 0] * from_left[6]
    window[14] = q[5]
    window[15] = q[6]
    window[16] = q[7] - own[0, 3] * from_right[7]
    window[17] = from_right[4] + share[1] - outer[0] * c1[3]
    window[18] = from_right[5]
    window[19] = from_right[6]
    for i in range(6):
        window[20 + i] = outer[2 + i]
    window[26] = c1[0]


def order(first, second, own, outer, out, mw, rw):
    for k, (source, coefficient) in enumerate(((first, mw), (second, rw))):
        for i in range(3):
            coefficient[i] = source[20 + i]
            coefficient[8 + i] = source[23 + i]
        for i in range(4):
            coefficient[3 + i] = own[k, i]
        coefficient[7] = outer[k]
    for i in range(20):
        out[i] = first[i]
    out[12] = first[12] - mw[2] * first[26]
    for i in range(7):
        out[20 + i] = second[2 + i]
    for i in range(5):
        out[27 + i] = second[13 + i]


def sweep(x0, q, mw, rw, last, levels, x1, x2, x3):
    def level(source, target, count, terms, shift):
        for i in range(count):
            mid = source[i + 1]
            force = half_force(mid, source[i], source[i + 2], mw[i + shift], rw[i + shift])
            target[i] = mid + force + q[terms + i]

    if x0 is not None:
        level(x0, x1, 11, 0, 0)
    level(x1, x2, 9, 11, 1)
    level(x2, x3, 7, 20, 2)
    level(x3, last, 5, 27, 3)
    if levels is not None:
        for i in range(5):
            levels[0, i] = x0[i + 4]
            levels[1, i] = x1[i + 3]
            levels[2, i] = x2[i + 2]
            levels[3, i] = x3[i + 1]
            levels[4, i] = last[i]


def first_kernel(flags, mine, other, own, outer, last, ordered, mw, rw, x2, x3):
    pl.when(flags[0] == 0)(lambda: order(mine, other, own, outer, ordered, mw, rw))
    pl.when(flags[0] != 0)(lambda: order(other, mine, own, outer, ordered, mw, rw))
    sweep(None, ordered, mw, rw, last, None, ordered.at[pl.ds(0, 11)], x2, x3)


def turn_kernel(turn, final, flags, ordered, mw, rw, mid, low, high, *refs):
    if turn > 1:
        kept, *refs = refs
    last, x0 = refs[:2]
    levels = refs[2] if final else None
    x1, x2, x3 = refs[-3:]

    @pl.when(flags[1] != turn)
    def _():
        for i in range(13):
            x0[i] = kept[i] if turn > 1 else jnp.zeros_like(x0[i])

    @pl.when(flags[1] == turn)
    def _():
        for i in range(4):
            x0[i] = low[i]
            x0[9 + i] = high[i]
        for i in range(5):
            x0[4 + i] = mid[i]

    sweep(x0, ordered, mw, rw, last, levels, x1, x2, x3)


def final_kernel(flags, start, b1, b2, b_before, b_late, b_later, levels, out, wide):
    core = flags[0]

    def corrected(m, b):
        for j in range(5):
            widen(levels[2 * core + m, j], wide, j)
        for j in range(4):
            low = wide[j]
            out[0, m, 2 * j] = b[2 * j] + low
            out[0, m, 2 * j + 1] = b[2 * j + 1] + 0.5 * (low + wide[j + 1])

    corrected(1, b1)
    corrected(2, b2)

    @pl.when(flags[2] == 0)
    def _():
        for i in range(8):
            out[0, 0, i] = start[i]

    pl.when(flags[2] == 2)(lambda: corrected(0, b_late))
    pl.when(flags[2] == 4)(lambda: corrected(0, b_later))
    pl.when((flags[2] != 0) & (flags[2] != 2) & (flags[2] != 4))(lambda: corrected(0, b_before))


def body(nodes, mobility, reaction):
    states = nodes[0]
    _, blocks, ny, nz = states.shape
    hy = ny // 2
    plane = (ny, nz)
    small = (hy, nz)
    slice_index = lax.axis_index("tm")
    flags = jnp.stack([slice_index % 2, slice_index // 2, slice_index]).astype(jnp.int32)

    own, to_right, to_left = pl.pallas_call(
        edge_kernel,
        out_shape=[jax.ShapeDtypeStruct(s, jnp.float32) for s in ((2, 4) + small, (10,) + plane, (10,) + plane)],
        in_specs=[pl.BlockSpec(memory_space=pltpu.SMEM)] + [pl.BlockSpec(memory_space=pltpu.HBM)] * 3,
        out_specs=[pl.BlockSpec(memory_space=pltpu.VMEM)] * 3,
        scratch_shapes=[pltpu.VMEM(s, jnp.float32) for s in (plane, (3, 8) + plane, (8,) + plane, (8,) + plane)]
        + [pltpu.SemaphoreType.DMA((8,))],
        compiler_params=pltpu.CompilerParams(vmem_limit_bytes=8 * 1024 * 1024),
        cost_estimate=cost(10**6, 4 * 10**6),
    )(flags, *(pltpu.with_memory_space_constraint(a, pltpu.HBM) for a in (states, mobility, reaction)))
    left = ring(to_right, "space", 1)
    right = ring(to_left, "space", -1)
    v1, step, first = call(
        local_kernel, [(8,) + plane] * 3, [(10,) + plane] * 3, states, mobility, reaction, flops=10**7
    )
    v1, v2, q, start, coarse, share, outer, to_right, to_left = call(
        fine_kernel,
        [(8,) + plane, (8,) + plane, (8,) + small, (5,) + small, (2, 4) + small, (2,) + small, (8,) + small, (9,) + small,
         (9,) + small],
        [(10,) + plane, (10,) + plane, (12,) + plane, (10,) + plane, (10,) + plane, (8,) + plane, (10,) + plane,
         (2, 8) + plane, (5,) + plane],
        flags, states, mobility, reaction, left, right, to_right, to_left, own, v1, step, first,
        flops=2 * 10**7, limit=16, scalars=1,
    )
    q_left = ring(to_right, "space", 1)
    q_right = ring(to_left, "space", -1)
    b1, b2 = call(base_kernel, [(8,) + plane, (8,) + plane], [(5,) + plane], v1, v2, coarse, q_left, q_right)
    count = lax.axis_size("tm")
    b_before = lax.ppermute(b2, "tm", [(i, i + 1) for i in range(count - 1) if i not in (1, 3)])
    (mine,) = call(
        pack_kernel, [(27,) + small], [], flags, q, start, coarse[0], share, own, outer, q_left, q_right, scalars=1
    )
    other = swapped(mine)
    levels_shape = [(11,) + small, (9,) + small, (7,) + small]
    last, ordered, mw, rw = call(
        first_kernel, [(5,) + small, (32,) + small, (11,) + small, (11,) + small], levels_shape[1:],
        flags, mine, other, own, outer, scalars=1,
    )
    turns = lax.axis_size("tm") // 2
    for turn in range(1, turns):
        final = turn == turns - 1
        if turn == 2:
            last, b_later = together(last, b_later)
        if turn == 3:
            last, sent = together(last, b2)
            b_late = lax.ppermute(sent, "tm", [(1, 2)])
        mid = hop(last, turn)
        if turn == 1:
            mid, sent = together(mid, b2)
            b_later = lax.ppermute(sent, "tm", [(3, 4)])
        low = ring(mid[0:4], "space", 1)
        high = ring(mid[1:5], "space", -1)
        if turn == 1:
            low, high, b_before = together(low, high, b_before)
        last, kept, *levels = call(
            functools.partial(turn_kernel, turn, final),
            [(5,) + small, (13,) + small] + [(5, 5) + small] * final,
            levels_shape,
            flags, ordered, mw, rw, mid, low, high, *([kept] if turn > 1 else []), scalars=1,
        )
    (out,) = call(
        final_kernel, [(1, 3, 8) + plane], [(5,) + plane], flags, states[0], b1, b2, b_before, b_late, b_later, levels[0], scalars=1,
    )
    return out


def solution(mesh):
    return jax.shard_map(
        body,
        mesh=mesh,
        in_specs=(
            P("tm", None, "space", None, None),
            P("space", None, None),
            P("space", None, None),
        ),
        out_specs=P("tm", None, "space", None, None),
        check_vma=False,
    )
```

```python
import functools
import jax
import jax.numpy as jnp
from jax import lax
from jax.experimental import pallas as pl
from jax.experimental.pallas import tpu as pltpu
from jax.sharding import PartitionSpec as P

edge = 5.0 / 24.0
middle = 1.0 / 3.0
far = -1.0 / 24.0
substep = 0.5


def roll(values, amount, axis):
    return pltpu.roll(values, amount % values.shape[axis], axis)


def around(values):
    return roll(values, 1, 0) + roll(values, -1, 0) + roll(values, 1, 1) + roll(values, -1, 1)


def cubic(values):
    return values - values * values * values


def cost(flops, moved):
    return pl.CostEstimate(flops=flops, bytes_accessed=moved, transcendentals=0)


def ring(values, axis, distance):
    count = lax.axis_size(axis)
    return lax.ppermute(values, axis, [(i, (i + distance) % count) for i in range(count)])


def together(*values):
    return lax.optimization_barrier(values)


def hop(values, turn):
    return lax.ppermute(values, "tm", [(2 * turn - 2 + core, 2 * turn + core) for core in range(2)])


def swapped(values):
    count = lax.axis_size("tm")
    return lax.ppermute(values, "tm", [(i, i ^ 1) for i in range(count)])


def call(kernel, outs, scratch, *args, flops=10**6, scalars=0, limit=8):
    moved = sum(a.size * 4 for a in args) + sum(4 * functools.reduce(lambda x, y: x * y, s) for s in outs)
    result = pl.pallas_call(
        kernel,
        out_shape=[jax.ShapeDtypeStruct(s, jnp.float32) for s in outs],
        in_specs=[pl.BlockSpec(memory_space=pltpu.SMEM)] * scalars
        + [pl.BlockSpec(memory_space=pltpu.VMEM)] * (len(args) - scalars),
        out_specs=[pl.BlockSpec(memory_space=pltpu.VMEM) for _ in outs],
        scratch_shapes=[pltpu.VMEM(s, jnp.float32) for s in scratch],
        compiler_params=pltpu.CompilerParams(vmem_limit_bytes=limit * 1024 * 1024),
        cost_estimate=cost(flops, moved),
    )(*args)
    return result


def laplace(mid, *beside):
    total = around(mid) - 6.0 * mid
    for values in beside:
        total = total + values
    return total


def leading(x0, x1, x2):
    return edge * x0 + middle * x1 + far * x2


def trailing(x0, x1, x2):
    return far * x0 + (middle - substep) * x1 + edge * x2


def cubics(nodes, plane):
    return [cubic(nodes[m, plane]) for m in range(3)]


def edge_kernel(flags, nodes_hbm, mob_hbm, rea_hbm, own, rightward, leftward, mix, nodes, mob, rea, sems):
    half = mob.shape[1] // 2
    copies = [pltpu.make_async_copy(mob_hbm, mob, sems.at[0]), pltpu.make_async_copy(rea_hbm, rea, sems.at[1])]
    for m in range(3):
        for k, first in enumerate((5, 0)):
            part = pl.ds(first, 3)
            copies.append(pltpu.make_async_copy(nodes_hbm.at[m, part], nodes.at[m, part], sems.at[2 + 2 * m + k]))
    for copy in copies:
        copy.start()
    for copy in copies[:2]:
        copy.wait()
    for k, (source, scale) in enumerate(((mob, 0.125), (rea, 0.5))):
        for j in range(4):
            own[k, j] = scale * source[2 * j, pl.ds(0, half, stride=2), :]

    for core in range(2):

        @pl.when(flags[0] == core)
        def _():
            for j in range(3):
                for out in (rightward, leftward):
                    out[8 + j // 2, pl.ds(j % 2 * half, half), :] = own[core, j + 1]

    for copy in copies[2:]:
        copy.wait()

    for out, outer, inner, third in ((rightward, 7, 6, 5), (leftward, 0, 1, 2)):
        lead = [leading(nodes[0, p], nodes[1, p], nodes[2, p]) for p in (outer, inner, third)]
        cubes = cubics(nodes, inner)
        out[0] = nodes[0, inner] + mob[inner] * laplace(lead[1], lead[0], lead[2]) + rea[inner] * leading(*cubes)
        cubes = cubics(nodes, outer)
        out[1] = nodes[0, outer] + mob[outer] * laplace(lead[0], lead[1]) + rea[outer] * leading(*cubes)
        out[4] = lead[0]
        trail = [trailing(nodes[0, p], nodes[1, p], nodes[2, p]) for p in (outer, inner)]
        out[2] = mob[outer] * laplace(trail[0], trail[1]) + rea[outer] * trailing(*cubes)
        out[5] = trail[0]
        out[3] = nodes[0, outer]
        out[6] = mob[outer]
        out[7] = rea[outer]
    mix[...] = 0.5 * nodes[0, 0] + 0.25 * nodes[0, 1]
    leftward[9, pl.ds(half, half), :] = reduced(mix)
    rightward[9, pl.ds(half, half), :] = jnp.zeros_like(own[0, 0])


def local_kernel(nodes, mob, rea, v1, step, first, lead, trail, start):
    for array in (lead, trail, start):
        for i in (0, 9):
            array[i] = jnp.zeros_like(array[i])

    @pl.loop(0, 8)
    def _(i):
        states = nodes[0, i], nodes[1, i], nodes[2, i]
        lead[i + 1] = leading(*states)
        trail[i + 1] = trailing(*states)
        start[i + 1] = states[0]

    @pl.loop(0, 8)
    def _(i):
        cubes = cubics(nodes, i)
        m = mob[i]
        r = rea[i]
        v1[i] = nodes[0, i] + m * laplace(lead[i + 1], lead[i], lead[i + 2]) + r * leading(*cubes)
        step[i] = m * laplace(trail[i + 1], trail[i], trail[i + 2]) + r * trailing(*cubes)
        first[i] = m * laplace(start[i + 1], start[i], start[i + 2]) + r * cubes[0]


def reduced(mix):
    half = mix.shape[0] // 2
    even = mix[pl.ds(0, half, stride=2), :]
    odd = mix[pl.ds(1, half, stride=2), :]
    return 0.5 * even + 0.25 * (odd + roll(odd, 1, 0))


def widen(d, wide, j):
    half = d.shape[0]
    wide[j, pl.ds(0, half, stride=2), :] = d
    wide[j, pl.ds(1, half, stride=2), :] = 0.5 * (d + roll(d, -1, 0))


def half_force(mid, low, high, mob, rea):
    planar = low + high + roll(mid, 1, 0) + roll(mid, -1, 0)
    vertical = roll(mid, 1, 1) + roll(mid, -1, 1)
    return mob * (planar + 4.0 * vertical - 12.0 * mid) + rea * cubic(mid)


def fine_kernel(
    flags, nodes, mob, rea, left, right, to_right, to_left, own, v1_own, step_own, first_own,
    v1_out, v2_out, q, start, coarse, share, outer, rightward, leftward,
    mw, rw, v1, v2, step, first, f1, jj, mix,
):
    half = mob.shape[1] // 2

    @pl.loop(0, 8)
    def _(i):
        mw[i + 1] = mob[i]
        rw[i + 1] = rea[i]
        v1[i + 2] = v1_own[i]
        step[i + 1] = step_own[i]
        first[i] = first_own[i]

    for got, sent, place, far_place, beyond, plane in ((left, to_left, 1, 0, 0, 0), (right, to_right, 10, 11, 9, 7)):
        mw[beyond] = got[6]
        rw[beyond] = got[7]
        v1[far_place] = got[0]
        v1[place] = got[1] + got[6] * sent[4]
        step[beyond] = got[2] + got[6] * sent[5]
        v1[plane + 2] = v1_own[plane] + mob[plane] * got[4]
        step[plane + 1] = step_own[plane] + mob[plane] * got[5]
        first[plane] = first_own[plane] + mob[plane] * got[3]

    @pl.loop(0, 10, unroll=2)
    def _(i):
        a = v1[i + 1]
        force = mw[i] * laplace(a, v1[i], v1[i + 2]) + rw[i] * cubic(a)
        f1[i] = force
        v2[i] = a + (substep * force + step[i])

    @pl.loop(0, 8, unroll=2)
    def _(i):
        a = v2[i + 1]
        force = mob[i] * laplace(a, v2[i], v2[i + 2]) + rea[i] * cubic(a)
        second = middle * f1[i + 1]
        v1_out[i] = v1[i + 2]
        v2_out[i] = a
        jj[0, i] = edge * first[i] + second + far * force
        jj[1, i] = far * first[i] + second + edge * force

    for j in range(4):
        before = nodes[0, 2 * j - 1] if j > 0 else left[3]
        mix[0] = 0.5 * nodes[0, 2 * j] + 0.25 * (nodes[0, 2 * j + 1] + before)
        mix[1] = 0.5 * v1[2 * j + 2] + 0.25 * (v1[2 * j + 3] + v1[2 * j + 1])
        mix[2] = 0.5 * v2[2 * j + 1] + 0.25 * (v2[2 * j + 2] + v2[2 * j])
        for m in range(2):
            mix[3 + m] = 0.5 * jj[m, 2 * j] + 0.25 * jj[m, 2 * j + 1]
            if j > 0:
                mix[3 + m] = mix[3 + m] + 0.25 * jj[m, 2 * j - 1]
        start[j] = reduced(mix.at[0])
        for m in range(2):
            coarse[m, j] = reduced(mix.at[1 + m])
            q[4 * m + j] = reduced(mix.at[3 + m])
    mix[0] = nodes[0, 7]
    start[4] = right[9, pl.ds(half, half), :] + 0.25 * reduced(mix.at[0])
    for m in range(2):
        mix[1 + m] = jj[m, 7]
        share[m] = 0.25 * reduced(mix.at[1 + m])

    outer[0] = 0.125 * right[6, pl.ds(0, half, stride=2), :]
    outer[1] = 0.5 * right[7, pl.ds(0, half, stride=2), :]
    for j in range(3):
        for side, got in enumerate((left, right)):
            outer[2 + 3 * side + j] = got[8 + j // 2, pl.ds(j % 2 * half, half), :]

    empty = jnp.zeros_like(share[0])

    @pl.when(flags[2] == 0)
    def _():
        for j in range(4):
            q[j] = q[j] + start[j]

    @pl.when(flags[2] != 0)
    def _():
        for j in range(4):
            low = start[j - 1] if j > 0 else empty
            q[j] = q[j] - half_force(start[j], low, start[j + 1], own[0, j], own[1, j])

    for j in range(4):
        low = coarse[0, j - 1] if j > 0 else empty
        high = coarse[0, j + 1] if j < 3 else empty
        q[4 + j] = q[4 + j] - half_force(coarse[0, j], low, high, own[0, j], own[1, j])

    for i in range(3):
        rightward[i] = q[1 + i]
        leftward[4 + i] = q[4 + i]
    for i in range(2):
        rightward[3 + i] = q[6 + i]
        rightward[7 + i] = share[i]
        leftward[7 + i] = coarse[i, 0]
    rightward[5] = start[3]
    rightward[6] = coarse[0, 3]
    for i in range(4):
        leftward[i] = q[i]


def base_kernel(v1, v2, coarse, from_left, from_right, b1, b2, mix):
    del from_left
    for m, v, b in ((0, v1, b1), (1, v2, b2)):
        for j in range(4):
            widen(coarse[m, j], mix, j)
        widen(from_right[7 + m], mix, 4)
        for j in range(4):
            low = mix[j]
            b[2 * j] = v[2 * j] - low
            b[2 * j + 1] = v[2 * j + 1] - 0.5 * (low + mix[j + 1])


def pack_kernel(flags, q, start, c1, share, own, outer, from_left, from_right, window):
    keep = jnp.where(flags[2] == 0, 0.0, 1.0)
    window[0] = from_left[0]
    window[1] = from_left[1]
    window[2] = from_left[2]
    window[3] = q[0] + from_left[7] - keep * own[0, 0] * from_left[5]
    for i in range(1, 4):
        window[3 + i] = q[i]
        window[7 + i] = from_right[i]
    window[7] = from_right[0] + share[0] - keep * outer[0] * start[3]
    window[11] = from_left[3]
    window[12] = from_left[4]
    window[13] = q[4] + from_left[8] - own[0, 0] * from_left[6]
    window[14] = q[5]
    window[15] = q[6]
    window[16] = q[7] - own[0, 3] * from_right[7]
    window[17] = from_right[4] + share[1] - outer[0] * c1[3]
    window[18] = from_right[5]
    window[19] = from_right[6]
    for i in range(6):
        window[20 + i] = outer[2 + i]
    window[26] = c1[0]


def order(first, second, own, outer, out, mw, rw):
    for k, (source, coefficient) in enumerate(((first, mw), (second, rw))):
        for i in range(3):
            coefficient[i] = source[20 + i]
            coefficient[8 + i] = source[23 + i]
        for i in range(4):
            coefficient[3 + i] = own[k, i]
        coefficient[7] = outer[k]
    for i in range(20):
        out[i] = first[i]
    out[12] = first[12] - mw[2] * first[26]
    for i in range(7):
        out[20 + i] = second[2 + i]
    for i in range(5):
        out[27 + i] = second[13 + i]


def sweep(x0, q, mw, rw, last, levels, x1, x2, x3):
    def level(source, target, count, terms, shift):
        for i in range(count):
            mid = source[i + 1]
            force = half_force(mid, source[i], source[i + 2], mw[i + shift], rw[i + shift])
            target[i] = mid + force + q[terms + i]

    if x0 is not None:
        level(x0, x1, 11, 0, 0)
    level(x1, x2, 9, 11, 1)
    level(x2, x3, 7, 20, 2)
    level(x3, last, 5, 27, 3)
    if levels is not None:
        for i in range(5):
            levels[0, i] = x0[i + 4]
            levels[1, i] = x1[i + 3]
            levels[2, i] = x2[i + 2]
            levels[3, i] = x3[i + 1]
            levels[4, i] = last[i]


def first_kernel(flags, mine, other, own, outer, last, ordered, mw, rw, x2, x3):
    pl.when(flags[0] == 0)(lambda: order(mine, other, own, outer, ordered, mw, rw))
    pl.when(flags[0] != 0)(lambda: order(other, mine, own, outer, ordered, mw, rw))
    sweep(None, ordered, mw, rw, last, None, ordered.at[pl.ds(0, 11)], x2, x3)


def turn_kernel(turn, final, flags, ordered, mw, rw, mid, low, high, *refs):
    if turn > 1:
        kept, *refs = refs
    last, x0 = refs[:2]
    levels = refs[2] if final else None
    x1, x2, x3 = refs[-3:]

    @pl.when(flags[1] != turn)
    def _():
        for i in range(13):
            x0[i] = kept[i] if turn > 1 else jnp.zeros_like(x0[i])

    @pl.when(flags[1] == turn)
    def _():
        for i in range(4):
            x0[i] = low[i]
            x0[9 + i] = high[i]
        for i in range(5):
            x0[4 + i] = mid[i]

    sweep(x0, ordered, mw, rw, last, levels, x1, x2, x3)


def final_kernel(flags, start, b1, b2, b_before, b_late, b_later, levels, out_hbm, out, wide, sems):
    core = flags[0]

    def corrected(m, b):
        for j in range(5):
            widen(levels[2 * core + m, j], wide, j)
        for j in range(4):
            low = wide[j]
            out[m, 2 * j] = b[2 * j] + low
            out[m, 2 * j + 1] = b[2 * j + 1] + 0.5 * (low + wide[j + 1])

    copies = [pltpu.make_async_copy(out.at[m], out_hbm.at[0, m], sems.at[m]) for m in range(3)]
    corrected(1, b1)
    copies[1].start()
    corrected(2, b2)
    copies[2].start()

    @pl.when(flags[2] == 0)
    def _():
        for i in range(8):
            out[0, i] = start[i]

    pl.when(flags[2] == 2)(lambda: corrected(0, b_late))
    pl.when(flags[2] == 4)(lambda: corrected(0, b_later))
    pl.when((flags[2] != 0) & (flags[2] != 2) & (flags[2] != 4))(lambda: corrected(0, b_before))
    copies[0].start()
    for copy in copies:
        copy.wait()


def closing_kernel(turn, flags, ordered, mw, rw, mid, low, high, kept, *refs):
    bases, (out_hbm, last, x0, levels, x1, x2, x3, out, wide, sems) = refs[:6], refs[6:]
    turn_kernel(turn, True, flags, ordered, mw, rw, mid, low, high, kept, last, x0, levels, x1, x2, x3)
    final_kernel(flags, *bases, levels, out_hbm, out, wide, sems)


def body(nodes, mobility, reaction):
    states = nodes[0]
    _, blocks, ny, nz = states.shape
    hy = ny // 2
    plane = (ny, nz)
    small = (hy, nz)
    slice_index = lax.axis_index("tm")
    flags = jnp.stack([slice_index % 2, slice_index // 2, slice_index]).astype(jnp.int32)

    own, to_right, to_left = pl.pallas_call(
        edge_kernel,
        out_shape=[jax.ShapeDtypeStruct(s, jnp.float32) for s in ((2, 4) + small, (10,) + plane, (10,) + plane)],
        in_specs=[pl.BlockSpec(memory_space=pltpu.SMEM)] + [pl.BlockSpec(memory_space=pltpu.HBM)] * 3,
        out_specs=[pl.BlockSpec(memory_space=pltpu.VMEM)] * 3,
        scratch_shapes=[pltpu.VMEM(s, jnp.float32) for s in (plane, (3, 8) + plane, (8,) + plane, (8,) + plane)]
        + [pltpu.SemaphoreType.DMA((8,))],
        compiler_params=pltpu.CompilerParams(vmem_limit_bytes=8 * 1024 * 1024),
        cost_estimate=cost(10**6, 4 * 10**6),
    )(flags, *(pltpu.with_memory_space_constraint(a, pltpu.HBM) for a in (states, mobility, reaction)))
    left = ring(to_right, "space", 1)
    right = ring(to_left, "space", -1)
    v1, step, first = call(
        local_kernel, [(8,) + plane] * 3, [(10,) + plane] * 3, states, mobility, reaction, flops=10**7
    )
    v1, v2, q, start, coarse, share, outer, to_right, to_left = call(
        fine_kernel,
        [(8,) + plane, (8,) + plane, (8,) + small, (5,) + small, (2, 4) + small, (2,) + small, (8,) + small, (9,) + small,
         (9,) + small],
        [(10,) + plane, (10,) + plane, (12,) + plane, (10,) + plane, (10,) + plane, (8,) + plane, (10,) + plane,
         (2, 8) + plane, (5,) + plane],
        flags, states, mobility, reaction, left, right, to_right, to_left, own, v1, step, first,
        flops=2 * 10**7, limit=16, scalars=1,
    )
    q_left = ring(to_right, "space", 1)
    q_right = ring(to_left, "space", -1)
    b1, b2 = call(base_kernel, [(8,) + plane, (8,) + plane], [(5,) + plane], v1, v2, coarse, q_left, q_right)
    count = lax.axis_size("tm")
    b_before = lax.ppermute(b2, "tm", [(i, i + 1) for i in range(count - 1) if i not in (1, 3)])
    (mine,) = call(
        pack_kernel, [(27,) + small], [], flags, q, start, coarse[0], share, own, outer, q_left, q_right, scalars=1
    )
    other = swapped(mine)
    levels_shape = [(11,) + small, (9,) + small, (7,) + small]
    last, ordered, mw, rw = call(
        first_kernel, [(5,) + small, (32,) + small, (11,) + small, (11,) + small], levels_shape[1:],
        flags, mine, other, own, outer, scalars=1,
    )
    turns = lax.axis_size("tm") // 2
    for turn in range(1, turns):
        final = turn == turns - 1
        if turn == 2:
            last, b_later = together(last, b_later)
        if turn == 3:
            last, sent = together(last, b2)
            b_late = lax.ppermute(sent, "tm", [(1, 2)])
        mid = hop(last, turn)
        if turn == 1:
            mid, sent = together(mid, b2)
            b_later = lax.ppermute(sent, "tm", [(3, 4)])
        low = ring(mid[0:4], "space", 1)
        high = ring(mid[1:5], "space", -1)
        if turn == 1:
            low, high, b_before = together(low, high, b_before)
        operands = (flags, ordered, mw, rw, mid, low, high) + ((kept,) if turn > 1 else ())
        if not final:
            last, kept = call(
                functools.partial(turn_kernel, turn, False), [(5,) + small, (13,) + small], levels_shape, *operands, scalars=1
            )
    scratch = [(5,) + small, (13,) + small, (5, 5) + small] + levels_shape + [(3, 8) + plane, (5,) + plane]
    return pl.pallas_call(
        functools.partial(closing_kernel, turns - 1),
        out_shape=jax.ShapeDtypeStruct((1, 3, 8) + plane, jnp.float32),
        in_specs=[pl.BlockSpec(memory_space=pltpu.SMEM)] + [pl.BlockSpec(memory_space=pltpu.VMEM)] * 13,
        out_specs=pl.BlockSpec(memory_space=pltpu.HBM),
        scratch_shapes=[pltpu.VMEM(s, jnp.float32) for s in scratch] + [pltpu.SemaphoreType.DMA((3,))],
        compiler_params=pltpu.CompilerParams(vmem_limit_bytes=12 * 1024 * 1024),
        cost_estimate=cost(10**7, 8 * 10**6),
    )(*operands, states[0], b1, b2, b_before, b_late, b_later)


def solution(mesh):
    return jax.shard_map(
        body,
        mesh=mesh,
        in_specs=(
            P("tm", None, "space", None, None),
            P("space", None, None),
            P("space", None, None),
        ),
        out_specs=P("tm", None, "space", None, None),
        check_vma=False,
    )
```

```python
import functools
import jax
import jax.numpy as jnp
from jax import lax
from jax.experimental import pallas as pl
from jax.experimental.pallas import tpu as pltpu
from jax.sharding import PartitionSpec as P

edge = 5.0 / 24.0
middle = 1.0 / 3.0
far = -1.0 / 24.0
substep = 0.5


def roll(values, amount, axis):
    return pltpu.roll(values, amount % values.shape[axis], axis)


def around(values):
    return roll(values, 1, 0) + roll(values, -1, 0) + roll(values, 1, 1) + roll(values, -1, 1)


def cubic(values):
    return values - values * values * values


def cost(flops, moved):
    return pl.CostEstimate(flops=flops, bytes_accessed=moved, transcendentals=0)


def where():
    index = lax.axis_index("tm")
    return index & 1, index >> 1, index


def ring(values, axis, distance):
    count = lax.axis_size(axis)
    return lax.ppermute(values, axis, [(i, (i + distance) % count) for i in range(count)])


def together(*values):
    return lax.optimization_barrier(values)


def hop(values, turn):
    return lax.ppermute(values, "tm", [(2 * turn - 2 + core, 2 * turn + core) for core in range(2)])


def swapped(values):
    count = lax.axis_size("tm")
    return lax.ppermute(values, "tm", [(i, i ^ 1) for i in range(count)])


def call(kernel, outs, scratch, *args, flops=10**6, scalars=0, limit=8):
    moved = sum(a.size * 4 for a in args) + sum(4 * functools.reduce(lambda x, y: x * y, s) for s in outs)
    result = pl.pallas_call(
        kernel,
        out_shape=[jax.ShapeDtypeStruct(s, jnp.float32) for s in outs],
        in_specs=[pl.BlockSpec(memory_space=pltpu.SMEM)] * scalars
        + [pl.BlockSpec(memory_space=pltpu.VMEM)] * (len(args) - scalars),
        out_specs=[pl.BlockSpec(memory_space=pltpu.VMEM) for _ in outs],
        scratch_shapes=[pltpu.VMEM(s, jnp.float32) for s in scratch],
        compiler_params=pltpu.CompilerParams(vmem_limit_bytes=limit * 1024 * 1024),
        cost_estimate=cost(flops, moved),
    )(*args)
    return result


def laplace(mid, *beside):
    total = around(mid) - 6.0 * mid
    for values in beside:
        total = total + values
    return total


def leading(x0, x1, x2):
    return edge * x0 + middle * x1 + far * x2


def trailing(x0, x1, x2):
    return far * x0 + (middle - substep) * x1 + edge * x2


def cubics(nodes, plane):
    return [cubic(nodes[m, plane]) for m in range(3)]


def edge_kernel(nodes_hbm, mob_hbm, rea_hbm, own, rightward, leftward, mix, nodes, mob, rea, sems):
    flags = where()
    half = mob.shape[1] // 2
    copies = [pltpu.make_async_copy(mob_hbm, mob, sems.at[0]), pltpu.make_async_copy(rea_hbm, rea, sems.at[1])]
    for m in range(3):
        for k, first in enumerate((5, 0)):
            part = pl.ds(first, 3)
            copies.append(pltpu.make_async_copy(nodes_hbm.at[m, part], nodes.at[m, part], sems.at[2 + 2 * m + k]))
    for copy in copies:
        copy.start()
    for copy in copies[:2]:
        copy.wait()
    for k, (source, scale) in enumerate(((mob, 0.125), (rea, 0.5))):
        for j in range(4):
            own[k, j] = scale * source[2 * j, pl.ds(0, half, stride=2), :]

    for core in range(2):

        @pl.when(flags[0] == core)
        def _():
            for j in range(3):
                for out in (rightward, leftward):
                    out[8 + j // 2, pl.ds(j % 2 * half, half), :] = own[core, j + 1]

    for copy in copies[2:]:
        copy.wait()

    for out, outer, inner, third in ((rightward, 7, 6, 5), (leftward, 0, 1, 2)):
        lead = [leading(nodes[0, p], nodes[1, p], nodes[2, p]) for p in (outer, inner, third)]
        cubes = cubics(nodes, inner)
        out[0] = nodes[0, inner] + mob[inner] * laplace(lead[1], lead[0], lead[2]) + rea[inner] * leading(*cubes)
        cubes = cubics(nodes, outer)
        out[1] = nodes[0, outer] + mob[outer] * laplace(lead[0], lead[1]) + rea[outer] * leading(*cubes)
        out[4] = lead[0]
        trail = [trailing(nodes[0, p], nodes[1, p], nodes[2, p]) for p in (outer, inner)]
        out[2] = mob[outer] * laplace(trail[0], trail[1]) + rea[outer] * trailing(*cubes)
        out[5] = trail[0]
        out[3] = nodes[0, outer]
        out[6] = mob[outer]
        out[7] = rea[outer]
    mix[...] = 0.5 * nodes[0, 0] + 0.25 * nodes[0, 1]
    leftward[9, pl.ds(half, half), :] = reduced(mix)
    rightward[9, pl.ds(half, half), :] = jnp.zeros_like(own[0, 0])


def local_kernel(nodes, mob, rea, v1, step, first, lead, trail, start):
    for array in (lead, trail, start):
        for i in (0, 9):
            array[i] = jnp.zeros_like(array[i])

    @pl.loop(0, 8)
    def _(i):
        states = nodes[0, i], nodes[1, i], nodes[2, i]
        lead[i + 1] = leading(*states)
        trail[i + 1] = trailing(*states)
        start[i + 1] = states[0]

    @pl.loop(0, 8)
    def _(i):
        cubes = cubics(nodes, i)
        m = mob[i]
        r = rea[i]
        v1[i] = nodes[0, i] + m * laplace(lead[i + 1], lead[i], lead[i + 2]) + r * leading(*cubes)
        step[i] = m * laplace(trail[i + 1], trail[i], trail[i + 2]) + r * trailing(*cubes)
        first[i] = m * laplace(start[i + 1], start[i], start[i + 2]) + r * cubes[0]


def reduced(mix):
    half = mix.shape[0] // 2
    even = mix[pl.ds(0, half, stride=2), :]
    odd = mix[pl.ds(1, half, stride=2), :]
    return 0.5 * even + 0.25 * (odd + roll(odd, 1, 0))


def widen(d, wide, j):
    half = d.shape[0]
    wide[j, pl.ds(0, half, stride=2), :] = d
    wide[j, pl.ds(1, half, stride=2), :] = 0.5 * (d + roll(d, -1, 0))


def half_force(mid, low, high, mob, rea):
    planar = low + high + roll(mid, 1, 0) + roll(mid, -1, 0)
    vertical = roll(mid, 1, 1) + roll(mid, -1, 1)
    return mob * (planar + 4.0 * vertical - 12.0 * mid) + rea * cubic(mid)


def fine_kernel(
    nodes, mob, rea, left, right, to_right, to_left, own, v1_own, step_own, first_own,
    v1_out, v2_out, q, start, coarse, share, outer, rightward, leftward,
    mw, rw, v1, v2, step, first, f1, jj, mix,
):
    flags = where()
    half = mob.shape[1] // 2

    @pl.loop(0, 8)
    def _(i):
        mw[i + 1] = mob[i]
        rw[i + 1] = rea[i]
        v1[i + 2] = v1_own[i]
        step[i + 1] = step_own[i]
        first[i] = first_own[i]

    for got, sent, place, far_place, beyond, plane in ((left, to_left, 1, 0, 0, 0), (right, to_right, 10, 11, 9, 7)):
        mw[beyond] = got[6]
        rw[beyond] = got[7]
        v1[far_place] = got[0]
        v1[place] = got[1] + got[6] * sent[4]
        step[beyond] = got[2] + got[6] * sent[5]
        v1[plane + 2] = v1_own[plane] + mob[plane] * got[4]
        step[plane + 1] = step_own[plane] + mob[plane] * got[5]
        first[plane] = first_own[plane] + mob[plane] * got[3]

    @pl.loop(0, 10, unroll=2)
    def _(i):
        a = v1[i + 1]
        force = mw[i] * laplace(a, v1[i], v1[i + 2]) + rw[i] * cubic(a)
        f1[i] = force
        v2[i] = a + (substep * force + step[i])

    @pl.loop(0, 8, unroll=2)
    def _(i):
        a = v2[i + 1]
        force = mob[i] * laplace(a, v2[i], v2[i + 2]) + rea[i] * cubic(a)
        second = middle * f1[i + 1]
        v1_out[i] = v1[i + 2]
        v2_out[i] = a
        jj[0, i] = edge * first[i] + second + far * force
        jj[1, i] = far * first[i] + second + edge * force

    for j in range(4):
        before = nodes[0, 2 * j - 1] if j > 0 else left[3]
        mix[0] = 0.5 * nodes[0, 2 * j] + 0.25 * (nodes[0, 2 * j + 1] + before)
        mix[1] = 0.5 * v1[2 * j + 2] + 0.25 * (v1[2 * j + 3] + v1[2 * j + 1])
        mix[2] = 0.5 * v2[2 * j + 1] + 0.25 * (v2[2 * j + 2] + v2[2 * j])
        for m in range(2):
            mix[3 + m] = 0.5 * jj[m, 2 * j] + 0.25 * jj[m, 2 * j + 1]
            if j > 0:
                mix[3 + m] = mix[3 + m] + 0.25 * jj[m, 2 * j - 1]
        start[j] = reduced(mix.at[0])
        for m in range(2):
            coarse[m, j] = reduced(mix.at[1 + m])
            q[4 * m + j] = reduced(mix.at[3 + m])
    mix[0] = nodes[0, 7]
    start[4] = right[9, pl.ds(half, half), :] + 0.25 * reduced(mix.at[0])
    for m in range(2):
        mix[1 + m] = jj[m, 7]
        share[m] = 0.25 * reduced(mix.at[1 + m])

    outer[0] = 0.125 * right[6, pl.ds(0, half, stride=2), :]
    outer[1] = 0.5 * right[7, pl.ds(0, half, stride=2), :]
    for j in range(3):
        for side, got in enumerate((left, right)):
            outer[2 + 3 * side + j] = got[8 + j // 2, pl.ds(j % 2 * half, half), :]

    empty = jnp.zeros_like(share[0])

    @pl.when(flags[2] == 0)
    def _():
        for j in range(4):
            q[j] = q[j] + start[j]

    @pl.when(flags[2] != 0)
    def _():
        for j in range(4):
            low = start[j - 1] if j > 0 else empty
            q[j] = q[j] - half_force(start[j], low, start[j + 1], own[0, j], own[1, j])

    for j in range(4):
        low = coarse[0, j - 1] if j > 0 else empty
        high = coarse[0, j + 1] if j < 3 else empty
        q[4 + j] = q[4 + j] - half_force(coarse[0, j], low, high, own[0, j], own[1, j])

    for i in range(3):
        rightward[i] = q[1 + i]
        leftward[4 + i] = q[4 + i]
    for i in range(2):
        rightward[3 + i] = q[6 + i]
        rightward[7 + i] = share[i]
        leftward[7 + i] = coarse[i, 0]
    rightward[5] = start[3]
    rightward[6] = coarse[0, 3]
    for i in range(4):
        leftward[i] = q[i]


def base_kernel(v1, v2, coarse, from_left, from_right, b1, b2, mix):
    del from_left
    for m, v, b in ((0, v1, b1), (1, v2, b2)):
        for j in range(4):
            widen(coarse[m, j], mix, j)
        widen(from_right[7 + m], mix, 4)
        for j in range(4):
            low = mix[j]
            b[2 * j] = v[2 * j] - low
            b[2 * j + 1] = v[2 * j + 1] - 0.5 * (low + mix[j + 1])


def pack_kernel(q, start, c1, share, own, outer, from_left, from_right, window):
    keep = jnp.where(where()[2] == 0, 0.0, 1.0)
    window[0] = from_left[0]
    window[1] = from_left[1]
    window[2] = from_left[2]
    window[3] = q[0] + from_left[7] - keep * own[0, 0] * from_left[5]
    for i in range(1, 4):
        window[3 + i] = q[i]
        window[7 + i] = from_right[i]
    window[7] = from_right[0] + share[0] - keep * outer[0] * start[3]
    window[11] = from_left[3]
    window[12] = from_left[4]
    window[13] = q[4] + from_left[8] - own[0, 0] * from_left[6]
    window[14] = q[5]
    window[15] = q[6]
    window[16] = q[7] - own[0, 3] * from_right[7]
    window[17] = from_right[4] + share[1] - outer[0] * c1[3]
    window[18] = from_right[5]
    window[19] = from_right[6]
    for i in range(6):
        window[20 + i] = outer[2 + i]
    window[26] = c1[0]


def order(first, second, own, outer, out, mw, rw):
    for k, (source, coefficient) in enumerate(((first, mw), (second, rw))):
        for i in range(3):
            coefficient[i] = source[20 + i]
            coefficient[8 + i] = source[23 + i]
        for i in range(4):
            coefficient[3 + i] = own[k, i]
        coefficient[7] = outer[k]
    for i in range(20):
        out[i] = first[i]
    out[12] = first[12] - mw[2] * first[26]
    for i in range(7):
        out[20 + i] = second[2 + i]
    for i in range(5):
        out[27 + i] = second[13 + i]


def sweep(x0, q, mw, rw, last, levels, x1, x2, x3):
    def level(source, target, count, terms, shift):
        for i in range(count):
            mid = source[i + 1]
            force = half_force(mid, source[i], source[i + 2], mw[i + shift], rw[i + shift])
            target[i] = mid + force + q[terms + i]

    if x0 is not None:
        level(x0, x1, 11, 0, 0)
    level(x1, x2, 9, 11, 1)
    level(x2, x3, 7, 20, 2)
    level(x3, last, 5, 27, 3)
    if levels is not None:
        for i in range(5):
            levels[0, i] = x0[i + 4]
            levels[1, i] = x1[i + 3]
            levels[2, i] = x2[i + 2]
            levels[3, i] = x3[i + 1]
            levels[4, i] = last[i]


def first_kernel(mine, other, own, outer, last, ordered, mw, rw, x2, x3):
    flags = where()
    pl.when(flags[0] == 0)(lambda: order(mine, other, own, outer, ordered, mw, rw))
    pl.when(flags[0] != 0)(lambda: order(other, mine, own, outer, ordered, mw, rw))
    sweep(None, ordered, mw, rw, last, None, ordered.at[pl.ds(0, 11)], x2, x3)


def turn_kernel(turn, final, ordered, mw, rw, mid, low, high, *refs):
    flags = where()
    if turn > 1:
        kept, *refs = refs
    last, x0 = refs[:2]
    levels = refs[2] if final else None
    x1, x2, x3 = refs[-3:]

    @pl.when(flags[1] != turn)
    def _():
        for i in range(13):
            x0[i] = kept[i] if turn > 1 else jnp.zeros_like(x0[i])

    @pl.when(flags[1] == turn)
    def _():
        for i in range(4):
            x0[i] = low[i]
            x0[9 + i] = high[i]
        for i in range(5):
            x0[4 + i] = mid[i]

    sweep(x0, ordered, mw, rw, last, levels, x1, x2, x3)


def final_kernel(start, b1, b2, b_before, b_late, b_later, levels, out_hbm, out, wide, sems):
    core = where()[0]

    def corrected(m, b):
        for j in range(5):
            widen(levels[2 * core + m, j], wide, j)
        for j in range(4):
            low = wide[j]
            out[m, 2 * j] = b[2 * j] + low
            out[m, 2 * j + 1] = b[2 * j + 1] + 0.5 * (low + wide[j + 1])

    flags = where()
    copies = [pltpu.make_async_copy(out.at[m], out_hbm.at[0, m], sems.at[m]) for m in range(3)]
    corrected(1, b1)
    copies[1].start()
    corrected(2, b2)
    copies[2].start()

    @pl.when(flags[2] == 0)
    def _():
        for i in range(8):
            out[0, i] = start[i]

    pl.when(flags[2] == 2)(lambda: corrected(0, b_late))
    pl.when(flags[2] == 4)(lambda: corrected(0, b_later))
    pl.when((flags[2] != 0) & (flags[2] != 2) & (flags[2] != 4))(lambda: corrected(0, b_before))
    copies[0].start()
    for copy in copies:
        copy.wait()


def closing_kernel(turn, ordered, mw, rw, mid, low, high, kept, *refs):
    bases, (out_hbm, last, x0, levels, x1, x2, x3, out, wide, sems) = refs[:6], refs[6:]
    turn_kernel(turn, True, ordered, mw, rw, mid, low, high, kept, last, x0, levels, x1, x2, x3)
    final_kernel(*bases, levels, out_hbm, out, wide, sems)


def body(nodes, mobility, reaction):
    states = nodes[0]
    _, blocks, ny, nz = states.shape
    hy = ny // 2
    plane = (ny, nz)
    small = (hy, nz)

    own, to_right, to_left = pl.pallas_call(
        edge_kernel,
        out_shape=[jax.ShapeDtypeStruct(s, jnp.float32) for s in ((2, 4) + small, (10,) + plane, (10,) + plane)],
        in_specs=[pl.BlockSpec(memory_space=pltpu.HBM)] * 3,
        out_specs=[pl.BlockSpec(memory_space=pltpu.VMEM)] * 3,
        scratch_shapes=[pltpu.VMEM(s, jnp.float32) for s in (plane, (3, 8) + plane, (8,) + plane, (8,) + plane)]
        + [pltpu.SemaphoreType.DMA((8,))],
        compiler_params=pltpu.CompilerParams(vmem_limit_bytes=8 * 1024 * 1024),
        cost_estimate=cost(10**6, 4 * 10**6),
    )(*(pltpu.with_memory_space_constraint(a, pltpu.HBM) for a in (states, mobility, reaction)))
    left = ring(to_right, "space", 1)
    right = ring(to_left, "space", -1)
    v1, step, first = call(
        local_kernel, [(8,) + plane] * 3, [(10,) + plane] * 3, states, mobility, reaction, flops=10**7
    )
    v1, v2, q, start, coarse, share, outer, to_right, to_left = call(
        fine_kernel,
        [(8,) + plane, (8,) + plane, (8,) + small, (5,) + small, (2, 4) + small, (2,) + small, (8,) + small, (9,) + small,
         (9,) + small],
        [(10,) + plane, (10,) + plane, (12,) + plane, (10,) + plane, (10,) + plane, (8,) + plane, (10,) + plane,
         (2, 8) + plane, (5,) + plane],
        states, mobility, reaction, left, right, to_right, to_left, own, v1, step, first,
        flops=2 * 10**7, limit=16,
    )
    q_left = ring(to_right, "space", 1)
    q_right = ring(to_left, "space", -1)
    b1, b2 = call(base_kernel, [(8,) + plane, (8,) + plane], [(5,) + plane], v1, v2, coarse, q_left, q_right)
    count = lax.axis_size("tm")
    b_before = lax.ppermute(b2, "tm", [(i, i + 1) for i in range(count - 1) if i not in (1, 3)])
    (mine,) = call(
        pack_kernel, [(27,) + small], [], q, start, coarse[0], share, own, outer, q_left, q_right
    )
    other = swapped(mine)
    levels_shape = [(11,) + small, (9,) + small, (7,) + small]
    last, ordered, mw, rw = call(
        first_kernel, [(5,) + small, (32,) + small, (11,) + small, (11,) + small], levels_shape[1:],
        mine, other, own, outer,
    )
    turns = lax.axis_size("tm") // 2
    for turn in range(1, turns):
        final = turn == turns - 1
        if turn == 2:
            last, b_later = together(last, b_later)
        if turn == 3:
            last, sent = together(last, b2)
            b_late = lax.ppermute(sent, "tm", [(1, 2)])
        mid = hop(last, turn)
        if turn == 1:
            mid, sent = together(mid, b2)
            b_later = lax.ppermute(sent, "tm", [(3, 4)])
        low = ring(mid[0:4], "space", 1)
        high = ring(mid[1:5], "space", -1)
        if turn == 1:
            low, high, b_before = together(low, high, b_before)
        operands = (ordered, mw, rw, mid, low, high) + ((kept,) if turn > 1 else ())
        if not final:
            last, kept = call(
                functools.partial(turn_kernel, turn, False), [(5,) + small, (13,) + small], levels_shape, *operands
            )
    scratch = [(5,) + small, (13,) + small, (5, 5) + small] + levels_shape + [(3, 8) + plane, (5,) + plane]
    return pl.pallas_call(
        functools.partial(closing_kernel, turns - 1),
        out_shape=jax.ShapeDtypeStruct((1, 3, 8) + plane, jnp.float32),
        in_specs=[pl.BlockSpec(memory_space=pltpu.VMEM)] * 13,
        out_specs=pl.BlockSpec(memory_space=pltpu.HBM),
        scratch_shapes=[pltpu.VMEM(s, jnp.float32) for s in scratch] + [pltpu.SemaphoreType.DMA((3,))],
        compiler_params=pltpu.CompilerParams(vmem_limit_bytes=12 * 1024 * 1024),
        cost_estimate=cost(10**7, 8 * 10**6),
    )(*operands, states[0], b1, b2, b_before, b_late, b_later)


def solution(mesh):
    return jax.shard_map(
        body,
        mesh=mesh,
        in_specs=(
            P("tm", None, "space", None, None),
            P("space", None, None),
            P("space", None, None),
        ),
        out_specs=P("tm", None, "space", None, None),
        check_vma=False,
    )
```

```python
import functools
import jax
import jax.numpy as jnp
from jax import lax
from jax.experimental import pallas as pl
from jax.experimental.pallas import tpu as pltpu
from jax.sharding import PartitionSpec as P

edge = 5.0 / 24.0
middle = 1.0 / 3.0
far = -1.0 / 24.0
substep = 0.5


def roll(values, amount, axis):
    return pltpu.roll(values, amount % values.shape[axis], axis)


def around(values):
    return roll(values, 1, 0) + roll(values, -1, 0) + roll(values, 1, 1) + roll(values, -1, 1)


def cubic(values):
    return values - values * values * values


def cost(flops, moved):
    return pl.CostEstimate(flops=flops, bytes_accessed=moved, transcendentals=0)


def where():
    index = lax.axis_index("tm")
    return index & 1, index >> 1, index


def ring(values, axis, distance):
    count = lax.axis_size(axis)
    return lax.ppermute(values, axis, [(i, (i + distance) % count) for i in range(count)])


def together(*values):
    return lax.optimization_barrier(values)


def hop(values, turn):
    return lax.ppermute(values, "tm", [(2 * turn - 2 + core, 2 * turn + core) for core in range(2)])


def swapped(values):
    count = lax.axis_size("tm")
    return lax.ppermute(values, "tm", [(i, i ^ 1) for i in range(count)])


def call(kernel, outs, scratch, *args, flops=10**6, scalars=0, limit=8):
    moved = sum(a.size * 4 for a in args) + sum(4 * functools.reduce(lambda x, y: x * y, s) for s in outs)
    result = pl.pallas_call(
        kernel,
        out_shape=[jax.ShapeDtypeStruct(s, jnp.float32) for s in outs],
        in_specs=[pl.BlockSpec(memory_space=pltpu.SMEM)] * scalars
        + [pl.BlockSpec(memory_space=pltpu.VMEM)] * (len(args) - scalars),
        out_specs=[pl.BlockSpec(memory_space=pltpu.VMEM) for _ in outs],
        scratch_shapes=[pltpu.VMEM(s, jnp.float32) for s in scratch],
        compiler_params=pltpu.CompilerParams(vmem_limit_bytes=limit * 1024 * 1024),
        cost_estimate=cost(flops, moved),
    )(*args)
    return result


def laplace(mid, *beside):
    total = around(mid) - 6.0 * mid
    for values in beside:
        total = total + values
    return total


def leading(x0, x1, x2):
    return edge * x0 + middle * x1 + far * x2


def trailing(x0, x1, x2):
    return far * x0 + (middle - substep) * x1 + edge * x2


def cubics(nodes, plane):
    return [cubic(nodes[m, plane]) for m in range(3)]


def edge_kernel(nodes_hbm, mob_hbm, rea_hbm, own, rightward, leftward, mix, nodes, mob, rea, sems):
    flags = where()
    half = mob.shape[1] // 2
    copies = [pltpu.make_async_copy(mob_hbm, mob, sems.at[0]), pltpu.make_async_copy(rea_hbm, rea, sems.at[1])]
    for m in range(3):
        for k, first in enumerate((5, 0)):
            part = pl.ds(first, 3)
            copies.append(pltpu.make_async_copy(nodes_hbm.at[m, part], nodes.at[m, part], sems.at[2 + 2 * m + k]))
    for copy in copies:
        copy.start()
    for copy in copies[:2]:
        copy.wait()
    for k, (source, scale) in enumerate(((mob, 0.125), (rea, 0.5))):
        for j in range(4):
            own[k, j] = scale * source[2 * j, pl.ds(0, half, stride=2), :]

    for core in range(2):

        @pl.when(flags[0] == core)
        def _():
            for j in range(3):
                for out in (rightward, leftward):
                    out[8 + j // 2, pl.ds(j % 2 * half, half), :] = own[core, j + 1]

    for copy in copies[2:]:
        copy.wait()

    for out, outer, inner, third in ((rightward, 7, 6, 5), (leftward, 0, 1, 2)):
        lead = [leading(nodes[0, p], nodes[1, p], nodes[2, p]) for p in (outer, inner, third)]
        cubes = cubics(nodes, inner)
        out[0] = nodes[0, inner] + mob[inner] * laplace(lead[1], lead[0], lead[2]) + rea[inner] * leading(*cubes)
        cubes = cubics(nodes, outer)
        out[1] = nodes[0, outer] + mob[outer] * laplace(lead[0], lead[1]) + rea[outer] * leading(*cubes)
        out[4] = lead[0]
        trail = [trailing(nodes[0, p], nodes[1, p], nodes[2, p]) for p in (outer, inner)]
        out[2] = mob[outer] * laplace(trail[0], trail[1]) + rea[outer] * trailing(*cubes)
        out[5] = trail[0]
        out[3] = nodes[0, outer]
        out[6] = mob[outer]
        out[7] = rea[outer]
    mix[...] = 0.5 * nodes[0, 0] + 0.25 * nodes[0, 1]
    leftward[9, pl.ds(half, half), :] = reduced(mix)
    rightward[9, pl.ds(half, half), :] = jnp.zeros_like(own[0, 0])


def local_kernel(nodes, mob, rea, v1, step, first, lead, trail, start):
    for array in (lead, trail, start):
        for i in (0, 9):
            array[i] = jnp.zeros_like(array[i])

    @pl.loop(0, 8)
    def _(i):
        states = nodes[0, i], nodes[1, i], nodes[2, i]
        lead[i + 1] = leading(*states)
        trail[i + 1] = trailing(*states)
        start[i + 1] = states[0]

    @pl.loop(0, 8)
    def _(i):
        cubes = cubics(nodes, i)
        m = mob[i]
        r = rea[i]
        v1[i] = nodes[0, i] + m * laplace(lead[i + 1], lead[i], lead[i + 2]) + r * leading(*cubes)
        step[i] = m * laplace(trail[i + 1], trail[i], trail[i + 2]) + r * trailing(*cubes)
        first[i] = m * laplace(start[i + 1], start[i], start[i + 2]) + r * cubes[0]


def reduced(mix):
    half = mix.shape[0] // 2
    even = mix[pl.ds(0, half, stride=2), :]
    odd = mix[pl.ds(1, half, stride=2), :]
    return 0.5 * even + 0.25 * (odd + roll(odd, 1, 0))


def widen(d, wide, j):
    half = d.shape[0]
    wide[j, pl.ds(0, half, stride=2), :] = d
    wide[j, pl.ds(1, half, stride=2), :] = 0.5 * (d + roll(d, -1, 0))


def half_force(mid, low, high, mob, rea):
    planar = low + high + roll(mid, 1, 0) + roll(mid, -1, 0)
    vertical = roll(mid, 1, 1) + roll(mid, -1, 1)
    return mob * (planar + 4.0 * vertical - 12.0 * mid) + rea * cubic(mid)


def fine_kernel(
    nodes, mob, rea, left, right, to_right, to_left, own, v1_own, step_own, first_own,
    v1_out, v2_out, q, start, coarse, share, outer, rightward, leftward,
    mw, rw, v1, v2, step, first, f1, jj, mix,
):
    flags = where()
    half = mob.shape[1] // 2

    @pl.loop(0, 8, unroll=4)
    def _(i):
        mw[i + 1] = mob[i]
        rw[i + 1] = rea[i]
        v1[i + 2] = v1_own[i]
        step[i + 1] = step_own[i]
        first[i] = first_own[i]

    for got, sent, place, far_place, beyond, plane in ((left, to_left, 1, 0, 0, 0), (right, to_right, 10, 11, 9, 7)):
        mw[beyond] = got[6]
        rw[beyond] = got[7]
        v1[far_place] = got[0]
        v1[place] = got[1] + got[6] * sent[4]
        step[beyond] = got[2] + got[6] * sent[5]
        v1[plane + 2] = v1_own[plane] + mob[plane] * got[4]
        step[plane + 1] = step_own[plane] + mob[plane] * got[5]
        first[plane] = first_own[plane] + mob[plane] * got[3]

    @pl.loop(0, 10, unroll=5)
    def _(i):
        a = v1[i + 1]
        force = mw[i] * laplace(a, v1[i], v1[i + 2]) + rw[i] * cubic(a)
        f1[i] = force
        v2[i] = a + (substep * force + step[i])

    @pl.loop(0, 8, unroll=4)
    def _(i):
        a = v2[i + 1]
        force = mob[i] * laplace(a, v2[i], v2[i + 2]) + rea[i] * cubic(a)
        second = middle * f1[i + 1]
        v1_out[i] = v1[i + 2]
        v2_out[i] = a
        jj[0, i] = edge * first[i] + second + far * force
        jj[1, i] = far * first[i] + second + edge * force

    for j in range(4):
        before = nodes[0, 2 * j - 1] if j > 0 else left[3]
        mix[0] = 0.5 * nodes[0, 2 * j] + 0.25 * (nodes[0, 2 * j + 1] + before)
        mix[1] = 0.5 * v1[2 * j + 2] + 0.25 * (v1[2 * j + 3] + v1[2 * j + 1])
        mix[2] = 0.5 * v2[2 * j + 1] + 0.25 * (v2[2 * j + 2] + v2[2 * j])
        for m in range(2):
            mix[3 + m] = 0.5 * jj[m, 2 * j] + 0.25 * jj[m, 2 * j + 1]
            if j > 0:
                mix[3 + m] = mix[3 + m] + 0.25 * jj[m, 2 * j - 1]
        start[j] = reduced(mix.at[0])
        for m in range(2):
            coarse[m, j] = reduced(mix.at[1 + m])
            q[4 * m + j] = reduced(mix.at[3 + m])
    mix[0] = nodes[0, 7]
    start[4] = right[9, pl.ds(half, half), :] + 0.25 * reduced(mix.at[0])
    for m in range(2):
        mix[1 + m] = jj[m, 7]
        share[m] = 0.25 * reduced(mix.at[1 + m])

    outer[0] = 0.125 * right[6, pl.ds(0, half, stride=2), :]
    outer[1] = 0.5 * right[7, pl.ds(0, half, stride=2), :]
    for j in range(3):
        for side, got in enumerate((left, right)):
            outer[2 + 3 * side + j] = got[8 + j // 2, pl.ds(j % 2 * half, half), :]

    empty = jnp.zeros_like(share[0])

    @pl.when(flags[2] == 0)
    def _():
        for j in range(4):
            q[j] = q[j] + start[j]

    @pl.when(flags[2] != 0)
    def _():
        for j in range(4):
            low = start[j - 1] if j > 0 else empty
            q[j] = q[j] - half_force(start[j], low, start[j + 1], own[0, j], own[1, j])

    for j in range(4):
        low = coarse[0, j - 1] if j > 0 else empty
        high = coarse[0, j + 1] if j < 3 else empty
        q[4 + j] = q[4 + j] - half_force(coarse[0, j], low, high, own[0, j], own[1, j])

    for i in range(3):
        rightward[i] = q[1 + i]
        leftward[4 + i] = q[4 + i]
    for i in range(2):
        rightward[3 + i] = q[6 + i]
        rightward[7 + i] = share[i]
        leftward[7 + i] = coarse[i, 0]
    rightward[5] = start[3]
    rightward[6] = coarse[0, 3]
    for i in range(4):
        leftward[i] = q[i]


def base_kernel(v1, v2, coarse, from_left, from_right, b1, b2, mix):
    del from_left
    for m, v, b in ((0, v1, b1), (1, v2, b2)):
        for j in range(4):
            widen(coarse[m, j], mix, j)
        widen(from_right[7 + m], mix, 4)
        for j in range(4):
            low = mix[j]
            b[2 * j] = v[2 * j] - low
            b[2 * j + 1] = v[2 * j + 1] - 0.5 * (low + mix[j + 1])


def pack_kernel(q, start, c1, share, own, outer, from_left, from_right, window):
    keep = jnp.where(where()[2] == 0, 0.0, 1.0)
    window[0] = from_left[0]
    window[1] = from_left[1]
    window[2] = from_left[2]
    window[3] = q[0] + from_left[7] - keep * own[0, 0] * from_left[5]
    for i in range(1, 4):
        window[3 + i] = q[i]
        window[7 + i] = from_right[i]
    window[7] = from_right[0] + share[0] - keep * outer[0] * start[3]
    window[11] = from_left[3]
    window[12] = from_left[4]
    window[13] = q[4] + from_left[8] - own[0, 0] * from_left[6]
    window[14] = q[5]
    window[15] = q[6]
    window[16] = q[7] - own[0, 3] * from_right[7]
    window[17] = from_right[4] + share[1] - outer[0] * c1[3]
    window[18] = from_right[5]
    window[19] = from_right[6]
    for i in range(6):
        window[20 + i] = outer[2 + i]
    window[26] = c1[0]


def order(first, second, own, outer, out, mw, rw):
    for k, (source, coefficient) in enumerate(((first, mw), (second, rw))):
        for i in range(3):
            coefficient[i] = source[20 + i]
            coefficient[8 + i] = source[23 + i]
        for i in range(4):
            coefficient[3 + i] = own[k, i]
        coefficient[7] = outer[k]
    for i in range(20):
        out[i] = first[i]
    out[12] = first[12] - mw[2] * first[26]
    for i in range(7):
        out[20 + i] = second[2 + i]
    for i in range(5):
        out[27 + i] = second[13 + i]


def sweep(x0, q, mw, rw, last, levels, x1, x2, x3):
    def level(source, target, count, terms, shift):
        for i in range(count):
            mid = source[i + 1]
            force = half_force(mid, source[i], source[i + 2], mw[i + shift], rw[i + shift])
            target[i] = mid + force + q[terms + i]

    if x0 is not None:
        level(x0, x1, 11, 0, 0)
    level(x1, x2, 9, 11, 1)
    level(x2, x3, 7, 20, 2)
    level(x3, last, 5, 27, 3)
    if levels is not None:
        for i in range(5):
            levels[0, i] = x0[i + 4]
            levels[1, i] = x1[i + 3]
            levels[2, i] = x2[i + 2]
            levels[3, i] = x3[i + 1]
            levels[4, i] = last[i]


def first_kernel(mine, other, own, outer, last, ordered, mw, rw, x2, x3):
    flags = where()
    pl.when(flags[0] == 0)(lambda: order(mine, other, own, outer, ordered, mw, rw))
    pl.when(flags[0] != 0)(lambda: order(other, mine, own, outer, ordered, mw, rw))
    sweep(None, ordered, mw, rw, last, None, ordered.at[pl.ds(0, 11)], x2, x3)


def turn_kernel(turn, final, ordered, mw, rw, mid, low, high, *refs):
    flags = where()
    if turn > 1:
        kept, *refs = refs
    last, x0 = refs[:2]
    levels = refs[2] if final else None
    x1, x2, x3 = refs[-3:]

    @pl.when(flags[1] != turn)
    def _():
        for i in range(13):
            x0[i] = kept[i] if turn > 1 else jnp.zeros_like(x0[i])

    @pl.when(flags[1] == turn)
    def _():
        for i in range(4):
            x0[i] = low[i]
            x0[9 + i] = high[i]
        for i in range(5):
            x0[4 + i] = mid[i]

    sweep(x0, ordered, mw, rw, last, levels, x1, x2, x3)


def final_kernel(start, b1, b2, b_before, b_late, b_later, levels, out_hbm, out, wide, sems):
    core = where()[0]

    def corrected(m, b):
        for j in range(5):
            widen(levels[2 * core + m, j], wide, j)
        for j in range(4):
            low = wide[j]
            out[m, 2 * j] = b[2 * j] + low
            out[m, 2 * j + 1] = b[2 * j + 1] + 0.5 * (low + wide[j + 1])

    flags = where()
    copies = [pltpu.make_async_copy(out.at[m], out_hbm.at[0, m], sems.at[m]) for m in range(3)]
    corrected(1, b1)
    copies[1].start()
    corrected(2, b2)
    copies[2].start()

    @pl.when(flags[2] == 0)
    def _():
        for i in range(8):
            out[0, i] = start[i]

    pl.when(flags[2] == 2)(lambda: corrected(0, b_late))
    pl.when(flags[2] == 4)(lambda: corrected(0, b_later))
    pl.when((flags[2] != 0) & (flags[2] != 2) & (flags[2] != 4))(lambda: corrected(0, b_before))
    copies[0].start()
    for copy in copies:
        copy.wait()


def closing_kernel(turn, ordered, mw, rw, mid, low, high, kept, *refs):
    bases, (out_hbm, last, x0, levels, x1, x2, x3, out, wide, sems) = refs[:6], refs[6:]
    turn_kernel(turn, True, ordered, mw, rw, mid, low, high, kept, last, x0, levels, x1, x2, x3)
    final_kernel(*bases, levels, out_hbm, out, wide, sems)


def body(nodes, mobility, reaction):
    states = nodes[0]
    _, blocks, ny, nz = states.shape
    hy = ny // 2
    plane = (ny, nz)
    small = (hy, nz)

    own, to_right, to_left = pl.pallas_call(
        edge_kernel,
        out_shape=[jax.ShapeDtypeStruct(s, jnp.float32) for s in ((2, 4) + small, (10,) + plane, (10,) + plane)],
        in_specs=[pl.BlockSpec(memory_space=pltpu.HBM)] * 3,
        out_specs=[pl.BlockSpec(memory_space=pltpu.VMEM)] * 3,
        scratch_shapes=[pltpu.VMEM(s, jnp.float32) for s in (plane, (3, 8) + plane, (8,) + plane, (8,) + plane)]
        + [pltpu.SemaphoreType.DMA((8,))],
        compiler_params=pltpu.CompilerParams(vmem_limit_bytes=8 * 1024 * 1024),
        cost_estimate=cost(10**6, 4 * 10**6),
    )(*(pltpu.with_memory_space_constraint(a, pltpu.HBM) for a in (states, mobility, reaction)))
    left = ring(to_right, "space", 1)
    right = ring(to_left, "space", -1)
    v1, step, first = call(
        local_kernel, [(8,) + plane] * 3, [(10,) + plane] * 3, states, mobility, reaction, flops=10**7
    )
    v1, v2, q, start, coarse, share, outer, to_right, to_left = call(
        fine_kernel,
        [(8,) + plane, (8,) + plane, (8,) + small, (5,) + small, (2, 4) + small, (2,) + small, (8,) + small, (9,) + small,
         (9,) + small],
        [(10,) + plane, (10,) + plane, (12,) + plane, (10,) + plane, (10,) + plane, (8,) + plane, (10,) + plane,
         (2, 8) + plane, (5,) + plane],
        states, mobility, reaction, left, right, to_right, to_left, own, v1, step, first,
        flops=2 * 10**7, limit=16,
    )
    q_left = ring(to_right, "space", 1)
    q_right = ring(to_left, "space", -1)
    b1, b2 = call(base_kernel, [(8,) + plane, (8,) + plane], [(5,) + plane], v1, v2, coarse, q_left, q_right)
    count = lax.axis_size("tm")
    b_before = lax.ppermute(b2, "tm", [(i, i + 1) for i in range(count - 1) if i not in (1, 3)])
    (mine,) = call(
        pack_kernel, [(27,) + small], [], q, start, coarse[0], share, own, outer, q_left, q_right
    )
    other = swapped(mine)
    levels_shape = [(11,) + small, (9,) + small, (7,) + small]
    last, ordered, mw, rw = call(
        first_kernel, [(5,) + small, (32,) + small, (11,) + small, (11,) + small], levels_shape[1:],
        mine, other, own, outer,
    )
    turns = lax.axis_size("tm") // 2
    for turn in range(1, turns):
        final = turn == turns - 1
        if turn == 2:
            last, b_later = together(last, b_later)
        if turn == 3:
            last, sent = together(last, b2)
            b_late = lax.ppermute(sent, "tm", [(1, 2)])
        mid = hop(last, turn)
        if turn == 1:
            mid, sent = together(mid, b2)
            b_later = lax.ppermute(sent, "tm", [(3, 4)])
        low = ring(mid[0:4], "space", 1)
        high = ring(mid[1:5], "space", -1)
        if turn == 1:
            low, high, b_before = together(low, high, b_before)
        operands = (ordered, mw, rw, mid, low, high) + ((kept,) if turn > 1 else ())
        if not final:
            last, kept = call(
                functools.partial(turn_kernel, turn, False), [(5,) + small, (13,) + small], levels_shape, *operands
            )
    scratch = [(5,) + small, (13,) + small, (5, 5) + small] + levels_shape + [(3, 8) + plane, (5,) + plane]
    return pl.pallas_call(
        functools.partial(closing_kernel, turns - 1),
        out_shape=jax.ShapeDtypeStruct((1, 3, 8) + plane, jnp.float32),
        in_specs=[pl.BlockSpec(memory_space=pltpu.VMEM)] * 13,
        out_specs=pl.BlockSpec(memory_space=pltpu.HBM),
        scratch_shapes=[pltpu.VMEM(s, jnp.float32) for s in scratch] + [pltpu.SemaphoreType.DMA((3,))],
        compiler_params=pltpu.CompilerParams(vmem_limit_bytes=12 * 1024 * 1024),
        cost_estimate=cost(10**7, 8 * 10**6),
    )(*operands, states[0], b1, b2, b_before, b_late, b_later)


def solution(mesh):
    return jax.shard_map(
        body,
        mesh=mesh,
        in_specs=(
            P("tm", None, "space", None, None),
            P("space", None, None),
            P("space", None, None),
        ),
        out_specs=P("tm", None, "space", None, None),
        check_vma=False,
    )
```
